32 devices in a mesh: band: 4 (over z), head: 4 (over y, x), dp: 2 (over core).
Axes of the slice: x: 2, y: 2, z: 4, core: 2. Of those that a mesh axis runs over, the one named last changes fastest.
Arguments:
- tokens: bfloat16 [32, 1024, 512], P(('dp', 'band'), None, 'head'), parts along dimension 0, may hold values from -6 to 6
- corner_row: int32 [2048], P('dp'), parts along dimension 0, may hold values from 0 to 14
- corner_col: int32 [2048], P('dp'), parts along dimension 0, may hold values from 0 to 1022
- fraction: float32 [2, 2048], P(None, 'dp'), parts along dimension 1, may hold values from 0 to 1
- w_query: bfloat16 [512, 512], P(None, 'head'), may hold values from -2 to 2
- w_key: bfloat16 [512, 512], P(None, 'head'), may hold values from -2 to 2
- w_value: bfloat16 [512, 512], P(None, 'head'), may hold values from -0.25 to 0.25
- w_out: bfloat16 [512, 512], P('head'), may hold values from -0.25 to 0.25
- conv_kernel: float32 [25, 512], P(None, 'head'), may hold values from -1.25 to 1.25
- norm_gain: float32 [512], replicated, may hold values from 0.1 to 1.9
Outputs:
- mixed: bfloat16 [32, 1024, 512], P(('dp', 'band'), None, 'head'), parts along dimension 0
The draws below stay inside these ranges and needn't reach their ends.
There are 2 independent parts, one for each index of `dp`. The reference program is written for one: setup_inputs(seed, part) draws one part's arguments, and reference() takes and returns one part's arrays. A program takes and returns all parts, laid end to end along the dimension named above; an argument that names none is the same for every part. Nothing has to cross between parts.
All inputs are finite; a program needn't handle non-finite values.
Results may differ from the reference program's by a relative error of at most 0.029.
Values may be sent and summed in bfloat16 or wider, within the bound.
A program may use at most 64 MiB of HBM per device.

```python
import math
import jax
import jax.numpy as jnp
import numpy as np
from jax import lax

D = 512
HEADS = 16
KER = 5
POINTS = 1024
W = 1024
HEAD_DIM = 32
H = 16
N_HEAD = 4


def paired_weight(key, salt):
    own = jax.random.normal(jax.random.fold_in(key, salt), (D, D), jnp.float32)
    values = own / D ** 0.5
    return jnp.clip(values, -2.0, 2.0).astype(jnp.bfloat16)


def draw_w_query(key, part):
    return paired_weight(key, 211)


def draw_w_key(key, part):
    return paired_weight(key, 307)


def plant(array, stream_key, smallest, top_value):
    extent = array.shape
    spot = [jax.random.randint(jax.random.fold_in(stream_key, axis), (), 0, extent[axis]) for axis in range(len(extent))]
    array = array.at[tuple(spot)].set(smallest)
    longest = extent.index(max(extent))
    spot[longest] = (spot[longest] + 1) % extent[longest]
    return array.at[tuple(spot)].set(top_value)


def steps_of(own_key, extent, cuts, low, largest):
    gain, own = 1.0, jax.random.fold_in(own_key, 6)
    for dim, blocks in cuts:
        draws = jnp.exp(jax.random.uniform(jax.random.fold_in(own, dim), (blocks,), jnp.float32, low / len(cuts), largest / len(cuts)))
        gain = gain * jnp.repeat(draws, extent[dim] // blocks).reshape([-1 if axis == dim else 1 for axis in range(len(extent))])
    return gain


def rank_table(amount, skew):
    loads = [(1 << 20) // math.isqrt(rank ** skew) + 1 for rank in range(1, amount + 1)]
    width = 1 + sum(loads) // (1 << 30)
    return np.cumsum(np.array([max(1, weight // width) for weight in loads]))


def ranked(key, dims, amount, lean):
    table = rank_table(amount, lean)
    ticket = jax.random.randint(jax.random.fold_in(key, 1), dims, 0, int(table[amount - 1]))
    standing = jnp.searchsorted(jnp.asarray(table, jnp.int32), ticket, side="right")
    return jax.random.permutation(jax.random.fold_in(key, 2), amount)[standing].astype(jnp.int32)


def scatter_about(rng, dims, scale, limit, split=(), held_as=jnp.bfloat16):
    level = steps_of(rng, dims, split, -0.22, 0.18) if split else 1.0
    values = jax.random.normal(rng, dims, jnp.float32) * scale * level
    return jnp.minimum(jnp.maximum(values, -limit), limit).astype(held_as)


def setup_inputs(seed: int = 0, part: int = 0) -> dict:
    key_list = jax.random.split(jax.random.key(seed), 11)
    part_keys = jax.random.split(jax.random.fold_in(key_list[10], part), 11)
    tokens = scatter_about(part_keys[0], (H, W, D), 1.0, 6.0, ((0, 4), (2, 4)))
    corner_row = plant(ranked(part_keys[1], (POINTS,), H - 1, 2), jax.random.fold_in(part_keys[1], 3), 0, (H - 1) - 1).astype(jnp.int32)
    corner_col = plant(jax.random.randint(part_keys[2], (POINTS,), 0, W - 1), jax.random.fold_in(part_keys[2], 1), 0, (W - 1) - 1).astype(jnp.int32)
    fraction = jnp.clip(jax.random.uniform(part_keys[3], (2, POINTS), jnp.float32, 0.0, 1.0), 0.0, 1.0)
    w_query = draw_w_query(jax.random.fold_in(key_list[10], 71), part)
    w_key = draw_w_key(jax.random.fold_in(key_list[10], 71), part)
    w_value = scatter_about(key_list[6], (D, D), D ** -0.5, 0.25, ((1, 4),))
    w_out = scatter_about(key_list[7], (D, D), D ** -0.5, 0.25, ((0, 4),))
    conv_kernel = scatter_about(key_list[8], (KER * KER, D), (KER * KER) ** -0.5, 1.25, ((1, 4),), jnp.float32)
    norm_gain = jnp.clip(1.0 + 0.18 * jax.random.normal(key_list[9], (D,), jnp.float32), 0.1, 1.9)
    return dict(tokens=tokens, corner_row=corner_row, corner_col=corner_col, fraction=fraction, w_query=w_query, w_key=w_key, w_value=w_value, w_out=w_out, conv_kernel=conv_kernel, norm_gain=norm_gain)


def layer_norm(values, norm_gain):
    values = values.astype(jnp.float32)
    center = lax.optimization_barrier(jnp.mean(values, axis=-1, keepdims=True))
    spread = lax.optimization_barrier(jnp.mean(jnp.square(values - center), axis=-1, keepdims=True))
    return ((values - center) * lax.rsqrt(spread + 1e-05) * norm_gain).astype(jnp.bfloat16)

def reference(tokens, corner_row, corner_col, fraction, w_query, w_key, w_value, w_out, conv_kernel, norm_gain):
    normed = layer_norm(tokens, norm_gain)
    count = H * W
    flat = normed.reshape(count, D)
    query = jnp.dot(flat, w_query, preferred_element_type=jnp.float32).astype(jnp.bfloat16)
    row_top = (1.0 - fraction[0]).astype(jnp.bfloat16).astype(jnp.float32)[:, None]
    row_bottom = fraction[0].astype(jnp.bfloat16).astype(jnp.float32)[:, None]
    col_left = (1.0 - fraction[1]).astype(jnp.bfloat16).astype(jnp.float32)[:, None]
    col_right = fraction[1].astype(jnp.bfloat16).astype(jnp.float32)[:, None]
    grid = normed.astype(jnp.float32)
    inner_top = col_left * grid[corner_row, corner_col] + col_right * grid[corner_row, corner_col + 1]
    inner_bottom = col_left * grid[corner_row + 1, corner_col] + col_right * grid[corner_row + 1, corner_col + 1]
    sampled = (row_top * inner_top + row_bottom * inner_bottom).astype(jnp.bfloat16)
    key = jnp.dot(sampled, w_key, preferred_element_type=jnp.float32).astype(jnp.bfloat16)
    value = jnp.dot(sampled, w_value, preferred_element_type=jnp.float32).astype(jnp.bfloat16)
    key_heads = key.reshape(POINTS, HEADS, HEAD_DIM).astype(jnp.float32)
    value_heads = value.reshape(POINTS, HEADS, HEAD_DIM).astype(jnp.float32)
    block = min(512, count)
    blocks = query.reshape(count // block, block, HEADS, HEAD_DIM)
    scale = 1.0 / HEAD_DIM ** 0.5

    def one_block(part):
        scores = jnp.einsum('qhd,khd->hqk', part.astype(jnp.float32), key_heads) * scale
        top = lax.optimization_barrier(jnp.max(scores, axis=-1, keepdims=True))
        expo = jnp.exp(scores - top)
        probs = (expo / lax.optimization_barrier(jnp.sum(expo, axis=-1, keepdims=True))).astype(jnp.bfloat16)
        out = jnp.einsum('hqk,khd->qhd', probs.astype(jnp.float32), value_heads)
        return out.astype(jnp.bfloat16).reshape(block, D)
    attended = lax.map(one_block, blocks).reshape(count, D)
    group = D // N_HEAD
    projected = jnp.zeros((count, D), jnp.float32)
    for index in range(N_HEAD):
        partial_sum = jnp.dot(attended[:, index * group:(index + 1) * group], w_out[index * group:(index + 1) * group], preferred_element_type=jnp.float32)
        partial_sum = lax.optimization_barrier(partial_sum.astype(jnp.bfloat16)).astype(jnp.float32)
        projected = projected + partial_sum
    margin = KER // 2
    padded = jnp.pad(grid, ((margin, margin), (margin, margin), (0, 0)))
    local = jnp.zeros((H, W, D), jnp.float32)
    for first in range(KER):
        for second in range(KER):
            local = local + conv_kernel[first * KER + second] * padded[first:first + H, second:second + W]
    total = tokens.astype(jnp.float32) + projected.reshape(H, W, D) + local
    return total.astype(jnp.bfloat16)
```

```python
import functools
import math

import jax
import jax.numpy as jnp
from jax import lax
from jax.experimental import pallas as pl
from jax.experimental.pallas import tpu as pltpu
from jax.sharding import PartitionSpec as P

HEADS = 16
KER = 5
EPS = 1e-05
BF = jnp.bfloat16
F32 = jnp.float32
VM = pl.BlockSpec(memory_space=pltpu.VMEM)


def params(**more):
    return pltpu.CompilerParams(vmem_limit_bytes=60 * 1024 * 1024, **more)


def dot(a, b, dims=((1,), (0,))):
    return lax.dot_general(a, b, (dims, ((), ())), preferred_element_type=F32)


def shift(me, off, count):
    return lax.rem(me + off, count)


def remote(src, dst, send, recv, where):
    return pltpu.make_async_remote_copy(
        src_ref=src,
        dst_ref=dst,
        send_sem=send,
        recv_sem=recv,
        device_id=where,
        device_id_type=pl.DeviceIdType.MESH,
    )


def greet(places):
    barrier = pltpu.get_barrier_semaphore()
    for where in places:
        pl.semaphore_signal(barrier, inc=1, device_id=where, device_id_type=pl.DeviceIdType.MESH)
    pl.semaphore_wait(barrier, len(places))


def stats_kernel(x_ref, out_ref):
    x = x_ref[0]
    channels = x.shape[1]
    part = 1.0 / channels
    mean = dot(x, jnp.full((channels, channels), part, BF))
    square = jnp.square(x.astype(F32) - mean)
    high = square.astype(BF)
    low = (square - high.astype(F32)).astype(BF)
    ones = jnp.ones((8, channels), BF)
    rows = ((1,), (1,))
    mean_row = dot(jnp.full((8, channels), part, BF), x, rows)
    spread_row = dot(ones, high, rows) + dot(ones, low, rows)
    out_ref[0:1, :] = mean_row[0:1]
    out_ref[1:2, :] = spread_row[0:1]


def local_stats(tokens):
    band_rows, columns, channels = tokens.shape
    return pl.pallas_call(
        stats_kernel,
        grid=(band_rows,),
        in_specs=[pl.BlockSpec((1, columns, channels), lambda i: (i, 0, 0))],
        out_specs=pl.BlockSpec((2, columns), lambda i: (0, i)),
        out_shape=jax.ShapeDtypeStruct((2, band_rows * columns), F32),
        compiler_params=params(),
        name="local_stats",
    )(tokens)


def first_kernel(n_head, n_band, margin, *refs):
    tok, stat, wq, wk, wv, wo = refs[:6]
    xs, stats, halo, gq, gk, gv, go = refs[6:13]
    send, recv, hsend, hrecv, dsend, drecv = refs[13:]
    head, band, dp = (lax.axis_index(name) for name in ("head", "band", "dp"))
    places = [{"head": shift(head, off, n_head)} for off in range(1, n_head)]
    places += [{"band": shift(band, 1, n_band)}, {"band": shift(band, n_band - 1, n_band)}]
    places += [{"dp": 1 - dp}]
    greet(places)
    rows = tok.shape[0]
    per_head = rows // n_head
    others = range(1, n_head)
    copies = {}
    for off in others:
        to = shift(head, off, n_head)
        pairs = [(stat, stats.at[head]), (tok.at[pl.ds(to * per_head, per_head)], xs.at[head])]
        for k, (src, dst) in enumerate(pairs):
            copies[k, off] = remote(src, dst, send.at[k, off - 1], recv.at[k, off - 1], {"head": to})
            copies[k, off].start()
    up = remote(
        tok.at[pl.ds(rows - margin, margin)], halo.at[0], hsend.at[0], hrecv.at[0],
        {"band": shift(band, 1, n_band)},
    )
    down = remote(
        tok.at[pl.ds(0, margin)], halo.at[1], hsend.at[1], hrecv.at[1],
        {"band": shift(band, n_band - 1, n_band)},
    )

    @pl.when(band < n_band - 1)
    def _():
        up.start()

    @pl.when(band > 0)
    def _():
        down.start()

    weights = [(wq, gq), (wk, gk), (wv, gv), (wo, go)]
    for off in others:
        to = shift(head, off, n_head)
        for k, (src, dst) in enumerate(weights):
            c = remote(src.at[dp], dst.at[dp, head], send.at[k + 2, off - 1], recv.at[k + 2, off - 1], {"head": to})
            copies[k + 2, off] = c
            c.start()
    xs[head] = tok[pl.ds(head * per_head, per_head)]
    stats[head] = stat[...]
    halves = []
    for src, dst in weights:
        dst[dp, head] = src[dp]
        dst[1 - dp, head] = src[1 - dp]
    for off in others:
        back = shift(head, n_head - off, n_head)
        for k, (src, dst) in enumerate(weights):
            copies[k + 2, off].wait_recv()
            c = remote(
                dst.at[dp, back], dst.at[dp, back], dsend.at[k, off - 1], drecv.at[k, off - 1],
                {"dp": 1 - dp},
            )
            c.start()
            halves.append(c)
    for off in others:
        for k in range(2):
            copies[k, off].wait()
        for k in range(4):
            copies[k + 2, off].wait_send()
    for c in halves:
        c.wait()

    @pl.when(band < n_band - 1)
    def _():
        up.wait_send()
        down.wait_recv()

    @pl.when(band > 0)
    def _():
        down.wait_send()
        up.wait_recv()


def first_exchange(tokens, stat, wq, wk, wv, wo, n_head, n_band):
    band_rows, columns, channels = tokens.shape
    margin = KER // 2
    halves = [w.reshape(2, w.shape[0] // 2, w.shape[1]) for w in (wq, wk, wv, wo)]
    outs = [
        jax.ShapeDtypeStruct((n_head, band_rows // n_head, columns, channels), tokens.dtype),
        jax.ShapeDtypeStruct((n_head,) + stat.shape, stat.dtype),
        jax.ShapeDtypeStruct((2, margin, columns, channels), tokens.dtype),
    ] + [jax.ShapeDtypeStruct((2, n_head) + w.shape[1:], w.dtype) for w in halves]
    sems = [pltpu.SemaphoreType.DMA((6, n_head - 1))] * 2
    sems += [pltpu.SemaphoreType.DMA((2,))] * 2
    sems += [pltpu.SemaphoreType.DMA((4, n_head - 1))] * 2
    return pl.pallas_call(
        functools.partial(first_kernel, n_head, n_band, margin),
        out_shape=outs,
        in_specs=[VM] * 6,
        out_specs=[VM] * 7,
        scratch_shapes=sems,
        compiler_params=params(collective_id=0, has_side_effects=True),
        name="first_exchange",
    )(tokens, stat, *halves)


def prepare_kernel(factor, n_head, n_band, tok, xs, stats, gain, cr, cc, fr, gq, normed, query, part, edge, wide, weight, comb, turned):
    rows, columns, channels = tok.shape
    head, band = lax.axis_index("head"), lax.axis_index("band")
    mean = stats[0, 0:1]
    for i in range(1, n_head):
        mean = mean + stats[i, 0:1]
    mean = mean * (1.0 / n_head)
    total = jnp.zeros_like(mean)
    for i in range(n_head):
        total = total + stats[i, 1:2] + channels * jnp.square(stats[i, 0:1] - mean)
    inv = lax.rsqrt(total * (1.0 / (n_head * channels)) + EPS)
    comb[...] = jnp.zeros_like(comb)
    comb[0:1, :] = mean
    comb[1:2, :] = inv
    margin = edge.shape[2] // columns
    edge[0] = comb[0:2, (rows - margin) * columns :]
    edge[1] = comb[0:2, : margin * columns]
    for r in range(rows):
        col = comb[:, r * columns : (r + 1) * columns].T
        value = ((tok[r].astype(F32) - col[:, 0:1]) * col[:, 1:2] * gain[head]).astype(BF)
        normed[r] = value
        turned[r * channels : (r + 1) * channels, :] = value.T
    per = xs.shape[1] * columns
    for r in range(xs.shape[1]):
        begin = pl.multiple_of(head * per + r * columns, 128)
        col = comb[:, pl.ds(begin, columns)].T
        for i in range(n_head):
            value = (xs[i, r].astype(F32) - col[:, 0:1]) * col[:, 1:2] * gain[i]
            wide[r * columns : (r + 1) * columns, i * channels : (i + 1) * channels] = value.astype(BF)
    half = gq.shape[2]
    for a in range(2):
        for i in range(n_head):
            weight[a * half : (a + 1) * half, i * channels : (i + 1) * channels] = gq[a, i]

    @pl.loop(0, per // 256)
    def _(step):
        at = pl.ds(pl.multiple_of(step * 256, 256), 256)
        query[at, :] = (dot(wide[at, :], weight[...]) * factor).astype(BF)

    left = (1.0 - fr[1:2]).astype(BF).astype(F32)
    right = fr[1:2].astype(BF).astype(F32)
    top = (1.0 - fr[0:1]).astype(BF).astype(F32)
    bottom = fr[0:1].astype(BF).astype(F32)
    points = cc.shape[1]
    share = channels // n_band
    block = 256

    for begin in range(0, points, block):
        at = slice(begin, begin + block)
        spot = lax.broadcasted_iota(jnp.int32, (columns, block), 0)
        table = jnp.where(
            spot == cc[:, at], left[:, at], jnp.where(spot == cc[:, at] + 1, right[:, at], 0.0)
        ).astype(BF)
        inner = dot(turned[...], table)
        total = jnp.zeros((channels, block), F32)
        for r in range(rows):
            row = band * rows + r
            w = jnp.where(cr[:, at] == row, top[:, at], 0.0) + jnp.where(
                cr[:, at] + 1 == row, bottom[:, at], 0.0
            )
            total = total + w * inner[r * channels : (r + 1) * channels]
        for b in range(n_band):
            part[b, :, at] = total[b * share : (b + 1) * share].astype(BF)


def prepare(tokens, xs, stats, gain, cr, cc, fr, gq, n_head, n_band, factor):
    rows, columns, channels = tokens.shape
    points = cc.shape[1]
    per = xs.shape[1] * columns
    width = n_head * channels
    margin = KER // 2
    return pl.pallas_call(
        functools.partial(prepare_kernel, factor, n_head, n_band),
        out_shape=[
            jax.ShapeDtypeStruct(tokens.shape, BF),
            jax.ShapeDtypeStruct((per, width), BF),
            jax.ShapeDtypeStruct((n_band, channels // n_band, points), BF),
            jax.ShapeDtypeStruct((2, 2, margin * columns), F32),
        ],
        in_specs=[VM] * 8,
        out_specs=[VM] * 4,
        scratch_shapes=[
            pltpu.VMEM((per, width), BF),
            pltpu.VMEM((width, width), BF),
            pltpu.VMEM((8, rows * columns), F32),
            pltpu.VMEM((rows * channels, columns), BF),
        ],
        compiler_params=params(),
        name="prepare",
    )(tokens, xs, stats, gain, cr, cc, fr, gq)


def second_kernel(n_head, n_band, part, edge, whole, rim, landed, bsend, brecv, esend, erecv, zsend, zrecv, hsend, hrecv):
    head, band = lax.axis_index("head"), lax.axis_index("band")
    places = [{"head": shift(head, off, n_head)} for off in range(1, n_head)]
    places += [{"band": shift(band, off, n_band)} for off in range(1, n_band)]
    greet(places)
    bands, heads = range(1, n_band), range(1, n_head)
    parts = []
    for off in bands:
        to = shift(band, off, n_band)
        c = remote(part.at[to], landed.at[off - 1], bsend.at[off - 1], brecv.at[off - 1], {"band": to})
        c.start()
        parts.append(c)
    up = remote(edge.at[0], rim.at[0], esend.at[0], erecv.at[0], {"band": shift(band, 1, n_band)})
    down = remote(
        edge.at[1], rim.at[1], esend.at[1], erecv.at[1], {"band": shift(band, n_band - 1, n_band)}
    )
    up.start()
    down.start()
    total = part[band].astype(F32)
    for off in bands:
        parts[off - 1].wait_recv()
        total = total + landed[off - 1].astype(F32)
    whole[band, head] = total.astype(BF)
    along, across = [], []
    for off in bands:
        c = remote(
            whole.at[band, head], whole.at[band, head], zsend.at[off - 1], zrecv.at[off - 1],
            {"band": shift(band, off, n_band)},
        )
        c.start()
        along.append(c)
    for step in range(n_band):
        source = shift(band, n_band - step, n_band)
        if step:
            along[step - 1].wait_recv()
        for off in heads:
            c = remote(
                whole.at[source, head], whole.at[source, head], hsend.at[step, off - 1],
                hrecv.at[step, off - 1], {"head": shift(head, off, n_head)},
            )
            c.start()
            across.append(c)
    for c in across:
        c.wait()
    for c in along + parts:
        c.wait_send()
    up.wait()
    down.wait()


def second_exchange(part, edge, n_head, n_band):
    sem = pltpu.SemaphoreType.DMA
    return pl.pallas_call(
        functools.partial(second_kernel, n_head, n_band),
        out_shape=[
            jax.ShapeDtypeStruct((n_band, n_head) + part.shape[1:], BF),
            jax.ShapeDtypeStruct(edge.shape, F32),
        ],
        in_specs=[VM] * 2,
        out_specs=[VM] * 2,
        scratch_shapes=[pltpu.VMEM((n_band - 1,) + part.shape[1:], BF)]
        + [sem((n_band - 1,))] * 2
        + [sem((2,))] * 2
        + [sem((n_band - 1,))] * 2
        + [sem((n_band, n_head - 1))] * 2,
        compiler_params=params(collective_id=1, has_side_effects=True),
        name="second_exchange",
    )(part, edge)


def attend_kernel(size, query, samples, gk, gv, go, out, sampled, turned, keys, values, weight, attended):
    n_band, n_head, share, points = samples.shape
    channels = share * n_band
    half = gk.shape[2]
    group = channels // size
    for b in range(n_band):
        for i in range(n_head):
            at = i * channels + b * share
            sampled[at : at + share, :] = samples[b, i]
    turned[...] = sampled[...].T
    low = go.shape[2]
    for a in range(2):
        for i in range(n_head):
            at = i * channels + a * low
            weight[at : at + low, :] = go[a, i]

    @pl.loop(0, n_head)
    def _(i):
        flip = ((0,), (0,))
        key = dot(gk[0, i], sampled[0:half, :], flip) + dot(gk[1, i], sampled[half:, :], flip)
        value = dot(turned[:, 0:half], gv[0, i]) + dot(turned[:, half:], gv[1, i])
        key_spot = lax.broadcasted_iota(jnp.int32, key.shape, 0)
        value_spot = lax.broadcasted_iota(jnp.int32, value.shape, 1)
        for j in range(group):
            low_end, high_end = j * size, (j + 1) * size
            keep = (key_spot >= low_end) & (key_spot < high_end)
            keys[i * group + j] = jnp.where(keep, key, 0.0).astype(BF)
            keep = (value_spot >= low_end) & (value_spot < high_end)
            values[i * group + j, :, 0:channels] = jnp.where(keep, value, 0.0).astype(BF)
            values[i * group + j, :, channels:] = jnp.ones((points, channels), BF)

    block = attended.shape[0]

    @pl.loop(0, query.shape[0] // block)
    def _(step):
        at = pl.ds(pl.multiple_of(step * block, block), block)

        @pl.loop(0, n_head)
        def _(i):
            lanes = pl.ds(pl.multiple_of(i * channels, channels), channels)
            q = query[at, lanes]
            total = jnp.zeros((block, channels), F32)
            for j in range(group):
                score = dot(q, keys[i * group + j])
                top = jnp.max(score, axis=1, keepdims=True)
                prob = jnp.exp2(score - top).astype(BF)
                both = dot(prob, values[i * group + j])
                total = total + both[:, 0:channels] / both[:, channels:]
            attended[:, lanes] = total.astype(BF)

        result = dot(attended[...], weight[...])
        for i in range(n_head):
            out[i, at, :] = result[:, i * channels : (i + 1) * channels].astype(BF)


def attend(query, samples, gk, gv, go):
    n_band, n_head, share, points = samples.shape
    count, width = query.shape
    channels = width // n_head
    return pl.pallas_call(
        functools.partial(attend_kernel, width // HEADS),
        out_shape=jax.ShapeDtypeStruct((n_head, count, channels), BF),
        in_specs=[VM] * 5,
        out_specs=VM,
        scratch_shapes=[
            pltpu.VMEM((width, points), BF),
            pltpu.VMEM((points, width), BF),
            pltpu.VMEM((HEADS, channels, points), BF),
            pltpu.VMEM((HEADS, points, 2 * channels), BF),
            pltpu.VMEM((width, width), BF),
            pltpu.VMEM((256, width), BF),
        ],
        compiler_params=params(),
        name="attend",
    )(query, samples, gk, gv, go)


def third_kernel(n_head, mine, out, send, recv):
    head = lax.axis_index("head")
    greet([{"head": shift(head, off, n_head)} for off in range(1, n_head)])
    copies = []
    for off in range(1, n_head):
        to = shift(head, off, n_head)
        c = remote(mine.at[to], out.at[head], send.at[off - 1], recv.at[off - 1], {"head": to})
        c.start()
        copies.append(c)
    out[head] = mine[head]
    for c in copies:
        c.wait()


def third_exchange(mine, n_head):
    return pl.pallas_call(
        functools.partial(third_kernel, n_head),
        out_shape=jax.ShapeDtypeStruct(mine.shape, BF),
        in_specs=[VM],
        out_specs=VM,
        scratch_shapes=[pltpu.SemaphoreType.DMA((n_head - 1,))] * 2,
        compiler_params=params(collective_id=2, has_side_effects=True),
        name="third_exchange",
    )(mine)


def mix_kernel(n_band, tok, normed, halo, rim, gain, taps, projected, out, padded, comb):
    rows, columns, channels = tok.shape
    margin = KER // 2
    head, band = lax.axis_index("head"), lax.axis_index("band")
    edge = 8
    padded[:, 0:edge, :] = jnp.zeros((rows + 2 * margin, edge, channels), F32)
    padded[:, edge + columns :, :] = jnp.zeros((rows + 2 * margin, edge, channels), F32)
    for r in range(rows):
        padded[margin + r, edge : edge + columns, :] = normed[r].astype(F32)
    for side in range(2):
        comb[...] = jnp.zeros_like(comb)
        comb[0:2, :] = rim[side]
        there = band > 0 if side == 0 else band < n_band - 1
        for r in range(margin):
            col = comb[:, r * columns : (r + 1) * columns].T
            value = (halo[side, r].astype(F32) - col[:, 0:1]) * col[:, 1:2] * gain[head]
            value = jnp.where(there, value.astype(BF).astype(F32), 0.0)
            padded[side * (margin + rows) + r, edge : edge + columns, :] = value
    block = 64

    @pl.loop(0, rows)
    def _(r):
        @pl.loop(0, columns // block)
        def _(step):
            begin = pl.multiple_of(step * block, block)
            at = pl.ds(begin, block)
            total = tok[r, at, :].astype(F32) + projected[r, at, :].astype(F32)
            for a in range(KER):
                for b in range(KER):
                    total = total + taps[a * KER + b : a * KER + b + 1, :] * padded[
                        r + a, pl.ds(begin + (edge - margin + b), block), :
                    ]
            out[r, at, :] = total.astype(BF)


def mix(tokens, normed, halo, rim, gain, taps, projected, n_band):
    rows, columns, channels = tokens.shape
    margin = KER // 2
    return pl.pallas_call(
        functools.partial(mix_kernel, n_band),
        out_shape=jax.ShapeDtypeStruct(tokens.shape, BF),
        in_specs=[VM] * 7,
        out_specs=VM,
        scratch_shapes=[
            pltpu.VMEM((rows + 2 * margin, columns + 16, channels), F32),
            pltpu.VMEM((8, margin * columns), F32),
        ],
        compiler_params=params(),
        name="mix",
    )(tokens, normed, halo, rim, gain, taps, projected)


def shards(
    tokens, corner_row, corner_col, fraction, w_query, w_key, w_value, w_out, conv_kernel, norm_gain
):
    n_head, n_band = lax.axis_size("head"), lax.axis_size("band")
    channels = tokens.shape[2]
    width = n_head * channels
    factor = math.log2(math.e) / math.sqrt(width // HEADS)
    gain = norm_gain.reshape(n_head, 1, channels)
    stat = local_stats(tokens)
    xs, stats, halo, gq, gk, gv, go = first_exchange(
        tokens, stat, w_query, w_key, w_value, w_out, n_head, n_band
    )
    normed, query, part, edge = prepare(
        tokens, xs, stats, gain, corner_row[None], corner_col[None], fraction, gq,
        n_head, n_band, factor,
    )
    samples, rim = second_exchange(part, edge, n_head, n_band)
    mine = attend(query, samples, gk, gv, go)
    projected = third_exchange(mine, n_head).reshape(tokens.shape)
    return mix(tokens, normed, halo, rim, gain, conv_kernel, projected, n_band)


def solution(mesh):
    return jax.shard_map(
        shards,
        mesh=mesh,
        in_specs=(
            P(("dp", "band"), None, "head"),
            P("dp"),
            P("dp"),
            P(None, "dp"),
            P(None, "head"),
            P(None, "head"),
            P(None, "head"),
            P("head", None),
            P(None, "head"),
            P(),
        ),
        out_specs=P(("dp", "band"), None, "head"),
        check_vma=False,
    )
```

```python
import functools
import math

import jax
import jax.numpy as jnp
from jax import lax
from jax.experimental import pallas as pl
from jax.experimental.pallas import tpu as pltpu
from jax.sharding import PartitionSpec as P

HEADS = 16
KER = 5
EPS = 1e-05
BF = jnp.bfloat16
F32 = jnp.float32
VM = pl.BlockSpec(memory_space=pltpu.VMEM)


def params(**more):
    return pltpu.CompilerParams(vmem_limit_bytes=60 * 1024 * 1024, **more)


def dot(a, b, dims=((1,), (0,))):
    return lax.dot_general(a, b, (dims, ((), ())), preferred_element_type=F32)


def shift(me, off, count):
    return lax.rem(me + off, count)


def remote(src, dst, send, recv, where):
    return pltpu.make_async_remote_copy(
        src_ref=src,
        dst_ref=dst,
        send_sem=send,
        recv_sem=recv,
        device_id=where,
        device_id_type=pl.DeviceIdType.MESH,
    )


def greet(places):
    barrier = pltpu.get_barrier_semaphore()
    for where in places:
        pl.semaphore_signal(barrier, inc=1, device_id=where, device_id_type=pl.DeviceIdType.MESH)
    pl.semaphore_wait(barrier, len(places))


def gather_start(pairs, head, dp, n_head, send, recv):
    copies = {}
    for off in range(1, n_head):
        to = shift(head, off, n_head)
        for k, (src, dst) in enumerate(pairs):
            c = remote(src.at[dp], dst.at[dp, head], send.at[k, off - 1], recv.at[k, off - 1], {"head": to})
            c.start()
            copies[k, off] = c
    for src, dst in pairs:
        dst[dp, head] = src[dp]
        dst[1 - dp, head] = src[1 - dp]
    return copies


def gather_relay(pairs, copies, head, dp, n_head, send, recv):
    halves = []
    for off in range(1, n_head):
        back = shift(head, n_head - off, n_head)
        for k, (src, dst) in enumerate(pairs):
            copies[k, off].wait_recv()
            c = remote(dst.at[dp, back], dst.at[dp, back], send.at[k, off - 1], recv.at[k, off - 1], {"dp": 1 - dp})
            c.start()
            halves.append(c)
    return halves


def gather_finish(copies, halves):
    for c in copies.values():
        c.wait_send()
    for c in halves:
        c.wait()


def gather_sems(count, n_head):
    return [pltpu.SemaphoreType.DMA((count, n_head - 1))] * 4


def halved(w):
    return w.reshape(2, w.shape[0] // 2, w.shape[1])


def stats_row(x):
    channels = x.shape[1]
    part = 1.0 / channels
    mean = dot(x, jnp.full((channels, channels), part, BF))
    square = jnp.square(x.astype(F32) - mean)
    high = square.astype(BF)
    low = (square - high.astype(F32)).astype(BF)
    ones = jnp.ones((8, channels), BF)
    rows = ((1,), (1,))
    mean_row = dot(jnp.full((8, channels), part, BF), x, rows)
    spread_row = dot(ones, high, rows) + dot(ones, low, rows)
    return mean_row[0:1], spread_row[0:1]


def first_kernel(n_head, n_band, margin, tok, xs, stats, halo, stat, send, recv, hsend, hrecv):
    head, band = lax.axis_index("head"), lax.axis_index("band")
    places = [{"head": shift(head, off, n_head)} for off in range(1, n_head)]
    places += [{"band": shift(band, 1, n_band)}, {"band": shift(band, n_band - 1, n_band)}]
    greet(places)
    rows, columns, channels = tok.shape
    per_head = rows // n_head
    others = range(1, n_head)
    copies = []
    for off in others:
        to = shift(head, off, n_head)
        c = remote(
            tok.at[pl.ds(to * per_head, per_head)], xs.at[head], send.at[0, off - 1],
            recv.at[0, off - 1], {"head": to},
        )
        c.start()
        copies.append(c)
    up = remote(
        tok.at[pl.ds(rows - margin, margin)], halo.at[0], hsend.at[0], hrecv.at[0],
        {"band": shift(band, 1, n_band)},
    )
    down = remote(
        tok.at[pl.ds(0, margin)], halo.at[1], hsend.at[1], hrecv.at[1],
        {"band": shift(band, n_band - 1, n_band)},
    )

    @pl.when(band < n_band - 1)
    def _():
        up.start()

    @pl.when(band > 0)
    def _():
        down.start()

    for r in range(rows):
        mean, spread = stats_row(tok[r])
        stat[0:1, r * columns : (r + 1) * columns] = mean
        stat[1:2, r * columns : (r + 1) * columns] = spread
    for off in others:
        to = shift(head, off, n_head)
        c = remote(stat, stats.at[head], send.at[1, off - 1], recv.at[1, off - 1], {"head": to})
        c.start()
        copies.append(c)
    xs[head] = tok[pl.ds(head * per_head, per_head)]
    stats[head] = stat[...]
    for c in copies:
        c.wait()

    @pl.when(band < n_band - 1)
    def _():
        up.wait_send()
        down.wait_recv()

    @pl.when(band > 0)
    def _():
        down.wait_send()
        up.wait_recv()


def first_exchange(tokens, n_head, n_band):
    band_rows, columns, channels = tokens.shape
    margin = KER // 2
    outs = [
        jax.ShapeDtypeStruct((n_head, band_rows // n_head, columns, channels), tokens.dtype),
        jax.ShapeDtypeStruct((n_head, 2, band_rows * columns), F32),
        jax.ShapeDtypeStruct((2, margin, columns, channels), tokens.dtype),
    ]
    sem = pltpu.SemaphoreType.DMA
    return pl.pallas_call(
        functools.partial(first_kernel, n_head, n_band, margin),
        out_shape=outs,
        in_specs=[VM],
        out_specs=[VM] * 3,
        scratch_shapes=[pltpu.VMEM((2, band_rows * columns), F32)]
        + [sem((2, n_head - 1))] * 2
        + [sem((2,))] * 2,
        compiler_params=params(collective_id=0, has_side_effects=True),
        name="first_exchange",
    )(tokens)


def prepare_kernel(n_head, n_band, tok, xs, stats, gain, cr, cc, fr, normed, wide, part, edge, comb, turned):
    rows, columns, channels = tok.shape
    head, band = lax.axis_index("head"), lax.axis_index("band")
    mean = stats[0, 0:1]
    for i in range(1, n_head):
        mean = mean + stats[i, 0:1]
    mean = mean * (1.0 / n_head)
    total = jnp.zeros_like(mean)
    for i in range(n_head):
        total = total + stats[i, 1:2] + channels * jnp.square(stats[i, 0:1] - mean)
    inv = lax.rsqrt(total * (1.0 / (n_head * channels)) + EPS)
    comb[...] = jnp.zeros_like(comb)
    comb[0:1, :] = mean
    comb[1:2, :] = inv
    margin = edge.shape[2] // columns
    edge[0] = comb[0:2, (rows - margin) * columns :]
    edge[1] = comb[0:2, : margin * columns]
    for r in range(rows):
        col = comb[:, r * columns : (r + 1) * columns].T
        value = ((tok[r].astype(F32) - col[:, 0:1]) * col[:, 1:2] * gain[head]).astype(BF)
        normed[r] = value
        turned[r * channels : (r + 1) * channels, :] = value.T
    per = xs.shape[1] * columns
    for r in range(xs.shape[1]):
        begin = pl.multiple_of(head * per + r * columns, 128)
        col = comb[:, pl.ds(begin, columns)].T
        for i in range(n_head):
            value = (xs[i, r].astype(F32) - col[:, 0:1]) * col[:, 1:2] * gain[i]
            wide[r * columns : (r + 1) * columns, i * channels : (i + 1) * channels] = value.astype(BF)
    left = (1.0 - fr[1:2]).astype(BF).astype(F32)
    right = fr[1:2].astype(BF).astype(F32)
    top = (1.0 - fr[0:1]).astype(BF).astype(F32)
    bottom = fr[0:1].astype(BF).astype(F32)
    points = cc.shape[1]
    share = channels // n_band
    block = 256

    for begin in range(0, points, block):
        at = slice(begin, begin + block)
        spot = lax.broadcasted_iota(jnp.int32, (columns, block), 0)
        table = jnp.where(
            spot == cc[:, at], left[:, at], jnp.where(spot == cc[:, at] + 1, right[:, at], 0.0)
        ).astype(BF)
        inner = dot(turned[...], table)
        total = jnp.zeros((channels, block), F32)
        for r in range(rows):
            row = band * rows + r
            w = jnp.where(cr[:, at] == row, top[:, at], 0.0) + jnp.where(
                cr[:, at] + 1 == row, bottom[:, at], 0.0
            )
            total = total + w * inner[r * channels : (r + 1) * channels]
        for b in range(n_band):
            part[b, :, at] = total[b * share : (b + 1) * share].astype(BF)


def prepare(tokens, xs, stats, gain, cr, cc, fr, n_head, n_band):
    rows, columns, channels = tokens.shape
    points = cc.shape[1]
    per = xs.shape[1] * columns
    width = n_head * channels
    margin = KER // 2
    return pl.pallas_call(
        functools.partial(prepare_kernel, n_head, n_band),
        out_shape=[
            jax.ShapeDtypeStruct(tokens.shape, BF),
            jax.ShapeDtypeStruct((per, width), BF),
            jax.ShapeDtypeStruct((n_band, channels // n_band, points), BF),
            jax.ShapeDtypeStruct((2, 2, margin * columns), F32),
        ],
        in_specs=[VM] * 7,
        out_specs=[VM] * 4,
        scratch_shapes=[
            pltpu.VMEM((8, rows * columns), F32),
            pltpu.VMEM((rows * channels, columns), BF),
        ],
        compiler_params=params(),
        name="prepare",
    )(tokens, xs, stats, gain, cr, cc, fr)


def second_kernel(
    factor, n_head, n_band,
    part, edge, tok, normed, halo, gain, taps, wide, wq, wk, wv,
    whole, base, query, gk, gv,
    landed, rim, padded, comb, gq, weight,
    bsend, brecv, esend, erecv, zsend, zrecv, hsend, hrecv, wsend, wrecv, dsend, drecv,
):
    head, band, dp = (lax.axis_index(name) for name in ("head", "band", "dp"))
    places = [{"head": shift(head, off, n_head)} for off in range(1, n_head)]
    places += [{"band": shift(band, off, n_band)} for off in range(1, n_band)]
    places += [{"dp": 1 - dp}]
    greet(places)
    bands, heads = range(1, n_band), range(1, n_head)
    up = remote(edge.at[0], rim.at[0], esend.at[0], erecv.at[0], {"band": shift(band, 1, n_band)})
    down = remote(
        edge.at[1], rim.at[1], esend.at[1], erecv.at[1], {"band": shift(band, n_band - 1, n_band)}
    )
    up.start()
    down.start()
    parts = []
    for off in bands:
        to = shift(band, off, n_band)
        c = remote(part.at[to], landed.at[off - 1], bsend.at[off - 1], brecv.at[off - 1], {"band": to})
        c.start()
        parts.append(c)
    pairs = [(wq, gq), (wk, gk), (wv, gv)]
    copies = gather_start(pairs, head, dp, n_head, wsend, wrecv)

    rows, columns, channels = tok.shape
    margin = KER // 2
    side_pad = 8
    padded[:, 0:side_pad, :] = jnp.zeros((rows + 2 * margin, side_pad, channels), F32)
    padded[:, side_pad + columns :, :] = jnp.zeros((rows + 2 * margin, side_pad, channels), F32)
    for r in range(rows):
        padded[margin + r, side_pad : side_pad + columns, :] = normed[r].astype(F32)

    def fill(side):
        comb[...] = jnp.zeros_like(comb)
        comb[0:2, :] = rim[side]
        there = band > 0 if side == 0 else band < n_band - 1
        for r in range(margin):
            col = comb[:, r * columns : (r + 1) * columns].T
            value = (halo[side, r].astype(F32) - col[:, 0:1]) * col[:, 1:2] * gain[head]
            value = jnp.where(there, value.astype(BF).astype(F32), 0.0)
            padded[side * (margin + rows) + r, side_pad : side_pad + columns, :] = value

    block = 64

    def convolve(first, last):
        @pl.loop(first, last)
        def _(r):
            @pl.loop(0, columns // block)
            def _(step):
                begin = pl.multiple_of(step * block, block)
                at = pl.ds(begin, block)
                total = tok[r, at, :].astype(F32)
                for a in range(KER):
                    for b in range(KER):
                        total = total + taps[a * KER + b : a * KER + b + 1, :] * padded[
                            r + a, pl.ds(begin + (side_pad - margin + b), block), :
                        ]
                base[r, at, :] = total

    up.wait()
    down.wait()
    fill(0)
    fill(1)
    convolve(0, rows // 4)

    total = part[band].astype(F32)
    for off in bands:
        parts[off - 1].wait_recv()
        total = total + landed[off - 1].astype(F32)
    whole[band, head] = total.astype(BF)
    along, across = [], []
    for off in bands:
        c = remote(
            whole.at[band, head], whole.at[band, head], zsend.at[off - 1], zrecv.at[off - 1],
            {"band": shift(band, off, n_band)},
        )
        c.start()
        along.append(c)
    for step in range(n_band):
        source = shift(band, n_band - step, n_band)
        if step == 1:
            convolve(rows // 4, rows // 2)
        if step == 2:
            halves = gather_relay(pairs, copies, head, dp, n_head, dsend, drecv)
        if step:
            along[step - 1].wait_recv()
        for off in heads:
            c = remote(
                whole.at[source, head], whole.at[source, head], hsend.at[step, off - 1],
                hrecv.at[step, off - 1], {"head": shift(head, off, n_head)},
            )
            c.start()
            across.append(c)
    convolve(rows // 2, rows)
    gather_finish(copies, halves)
    half = gq.shape[2]
    for a in range(2):
        for i in range(n_head):
            weight[a * half : (a + 1) * half, i * channels : (i + 1) * channels] = gq[a, i]

    @pl.loop(0, wide.shape[0] // 256)
    def _(step):
        at = pl.ds(pl.multiple_of(step * 256, 256), 256)
        query[at, :] = (dot(wide[at, :], weight[...]) * factor).astype(BF)

    for c in across:
        c.wait()
    for c in along + parts:
        c.wait_send()


def second_exchange(part, edge, tokens, normed, halo, gain, taps, wide, wq, wk, wv, n_head, n_band, factor):
    sem = pltpu.SemaphoreType.DMA
    rows, columns, channels = tokens.shape
    margin = KER // 2
    weights = [halved(w) for w in (wq, wk, wv)]
    gathered = [(2, n_head) + w.shape[1:] for w in weights]
    return pl.pallas_call(
        functools.partial(second_kernel, factor, n_head, n_band),
        out_shape=[
            jax.ShapeDtypeStruct((n_band, n_head) + part.shape[1:], BF),
            jax.ShapeDtypeStruct(tokens.shape, F32),
            jax.ShapeDtypeStruct(wide.shape, BF),
            jax.ShapeDtypeStruct(gathered[1], BF),
            jax.ShapeDtypeStruct(gathered[2], BF),
        ],
        in_specs=[VM] * 11,
        out_specs=[VM] * 5,
        scratch_shapes=[
            pltpu.VMEM((n_band - 1,) + part.shape[1:], BF),
            pltpu.VMEM(edge.shape, F32),
            pltpu.VMEM((rows + 2 * margin, columns + 16, channels), F32),
            pltpu.VMEM((8, margin * columns), F32),
            pltpu.VMEM(gathered[0], BF),
            pltpu.VMEM((wide.shape[1], wide.shape[1]), BF),
        ]
        + [sem((n_band - 1,))] * 2
        + [sem((2,))] * 2
        + [sem((n_band - 1,))] * 2
        + [sem((n_band, n_head - 1))] * 2
        + gather_sems(3, n_head),
        compiler_params=params(collective_id=1, has_side_effects=True),
        name="second_exchange",
    )(part, edge, tokens, normed, halo, gain, taps, wide, *weights)


def attend_kernel(
    size, query, samples, gk, gv, wo, base, out,
    sampled, turned, keys, values, go, weight, attended, mine, landed,
    send, recv, wsend, wrecv, dsend, drecv,
):
    n_band, n_head, share, points = samples.shape
    head, dp = lax.axis_index("head"), lax.axis_index("dp")
    greet([{"head": shift(head, off, n_head)} for off in range(1, n_head)] + [{"dp": 1 - dp}])
    pairs = [(wo, go)]
    copies = gather_start(pairs, head, dp, n_head, wsend, wrecv)
    channels = share * n_band
    half = gk.shape[2]
    group = channels // size
    for b in range(n_band):
        for i in range(n_head):
            at = i * channels + b * share
            sampled[at : at + share, :] = samples[b, i]
    turned[...] = sampled[...].T

    @pl.loop(0, n_head)
    def _(i):
        flip = ((0,), (0,))
        key = dot(gk[0, i], sampled[0:half, :], flip) + dot(gk[1, i], sampled[half:, :], flip)
        value = dot(turned[:, 0:half], gv[0, i]) + dot(turned[:, half:], gv[1, i])
        key_spot = lax.broadcasted_iota(jnp.int32, key.shape, 0)
        value_spot = lax.broadcasted_iota(jnp.int32, value.shape, 1)
        for j in range(group):
            low_end, high_end = j * size, (j + 1) * size
            keep = (key_spot >= low_end) & (key_spot < high_end)
            keys[i * group + j] = jnp.where(keep, key, 0.0).astype(BF)
            keep = (value_spot >= low_end) & (value_spot < high_end)
            values[i * group + j, :, 0:channels] = jnp.where(keep, value, 0.0).astype(BF)
            values[i * group + j, :, channels:] = jnp.ones((points, channels), BF)

    halves = gather_relay(pairs, copies, head, dp, n_head, dsend, drecv)
    gather_finish(copies, halves)
    low = go.shape[2]
    for a in range(2):
        for i in range(n_head):
            at = i * channels + a * low
            weight[at : at + low, :] = go[a, i]
    block = attended.shape[0]
    steps = query.shape[0] // block

    def back(step, off):
        at = pl.ds(pl.multiple_of(step * block, block), block)
        to = shift(head, off, n_head)
        return remote(
            mine.at[to, at], landed.at[head, at], send.at[step, off - 1], recv.at[step, off - 1],
            {"head": to},
        )

    @pl.loop(0, steps)
    def _(step):
        at = pl.ds(pl.multiple_of(step * block, block), block)

        def score(h):
            i = h // group
            return dot(query[at, i * channels : (i + 1) * channels], keys[h])

        following = score(0)
        for i in range(n_head):
            total = jnp.zeros((block, channels), F32)
            for j in range(group):
                h = i * group + j
                current = following
                if h + 1 < n_head * group:
                    following = score(h + 1)
                top = jnp.max(current, axis=1, keepdims=True)
                prob = jnp.exp2(current - top).astype(BF)
                both = dot(prob, values[h])
                total = total + both[:, 0:channels] / both[:, channels:]
            attended[:, i * channels : (i + 1) * channels] = total.astype(BF)
        result = dot(attended[...], weight[...])
        for i in range(n_head):
            mine[i, at, :] = result[:, i * channels : (i + 1) * channels].astype(BF)
        for off in range(1, n_head):
            back(step, off).start()

    out[head] = (base[head] + mine[head].astype(F32)).astype(BF)
    for off in range(1, n_head):
        source = shift(head, n_head - off, n_head)
        for step in range(steps):
            back(step, off).wait()
        out[source] = (base[source] + landed[source].astype(F32)).astype(BF)


def attend(query, samples, gk, gv, wo, base):
    n_band, n_head, share, points = samples.shape
    count, width = query.shape
    channels = width // n_head
    block = 256
    wo = halved(wo)
    base = base.reshape(n_head, count, channels)
    return pl.pallas_call(
        functools.partial(attend_kernel, width // HEADS),
        out_shape=jax.ShapeDtypeStruct((n_head, count, channels), BF),
        in_specs=[VM] * 6,
        out_specs=VM,
        scratch_shapes=[
            pltpu.VMEM((width, points), BF),
            pltpu.VMEM((points, width), BF),
            pltpu.VMEM((HEADS, channels, points), BF),
            pltpu.VMEM((HEADS, points, 2 * channels), BF),
            pltpu.VMEM((2, n_head) + wo.shape[1:], BF),
            pltpu.VMEM((width, width), BF),
            pltpu.VMEM((block, width), BF),
            pltpu.VMEM((n_head, count, channels), BF),
            pltpu.VMEM((n_head, count, channels), BF),
        ]
        + [pltpu.SemaphoreType.DMA((count // block, n_head - 1))] * 2
        + gather_sems(1, n_head),
        compiler_params=params(collective_id=2, has_side_effects=True),
        name="attend",
    )(query, samples, gk, gv, wo, base)


def shards(
    tokens, corner_row, corner_col, fraction, w_query, w_key, w_value, w_out, conv_kernel, norm_gain
):
    n_head, n_band = lax.axis_size("head"), lax.axis_size("band")
    channels = tokens.shape[2]
    width = n_head * channels
    factor = math.log2(math.e) / math.sqrt(width // HEADS)
    gain = norm_gain.reshape(n_head, 1, channels)
    xs, stats, halo = first_exchange(tokens, n_head, n_band)
    normed, wide, part, edge = prepare(
        tokens, xs, stats, gain, corner_row[None], corner_col[None], fraction, n_head, n_band
    )
    samples, base, query, gk, gv = second_exchange(
        part, edge, tokens, normed, halo, gain, conv_kernel, wide, w_query, w_key, w_value,
        n_head, n_band, factor,
    )
    return attend(query, samples, gk, gv, w_out, base).reshape(tokens.shape)


def solution(mesh):
    return jax.shard_map(
        shards,
        mesh=mesh,
        in_specs=(
            P(("dp", "band"), None, "head"),
            P("dp"),
            P("dp"),
            P(None, "dp"),
            P(None, "head"),
            P(None, "head"),
            P(None, "head"),
            P("head", None),
            P(None, "head"),
            P(),
        ),
        out_specs=P(("dp", "band"), None, "head"),
        check_vma=False,
    )
```

```python
import functools
import math

import jax
import jax.numpy as jnp
from jax import lax
from jax.experimental import pallas as pl
from jax.experimental.pallas import tpu as pltpu
from jax.sharding import PartitionSpec as P

HEADS = 16
KER = 5
EPS = 1e-05
BF = jnp.bfloat16
F32 = jnp.float32
VM = pl.BlockSpec(memory_space=pltpu.VMEM)


def params(**more):
    return pltpu.CompilerParams(vmem_limit_bytes=44 * 1024 * 1024, **more)


def dot(a, b, dims=((1,), (0,))):
    return lax.dot_general(a, b, (dims, ((), ())), preferred_element_type=F32)


def shift(me, off, count):
    return lax.rem(me + off, count)


def remote(src, dst, send, recv, where):
    return pltpu.make_async_remote_copy(
        src_ref=src,
        dst_ref=dst,
        send_sem=send,
        recv_sem=recv,
        device_id=where,
        device_id_type=pl.DeviceIdType.MESH,
    )


def greet(places):
    barrier = pltpu.get_barrier_semaphore()
    for where in places:
        pl.semaphore_signal(barrier, inc=1, device_id=where, device_id_type=pl.DeviceIdType.MESH)
    pl.semaphore_wait(barrier, len(places))


def gather_start(pairs, head, dp, n_head, sems):
    copies = {}
    for off in range(1, n_head):
        to = shift(head, off, n_head)
        for k, src, dst in pairs:
            c = remote(src.at[dp], dst.at[dp, head], sems[0].at[k, off - 1], sems[1].at[k, off - 1], {"head": to})
            c.start()
            copies[k, off] = c
    for k, src, dst in pairs:
        dst[dp, head] = src[dp]
        dst[1 - dp, head] = src[1 - dp]
    return copies


def gather_relay(pairs, copies, head, dp, n_head, sems):
    halves = []
    for off in range(1, n_head):
        back = shift(head, n_head - off, n_head)
        for k, src, dst in pairs:
            copies[k, off].wait_recv()
            c = remote(
                dst.at[dp, back], dst.at[dp, back], sems[2].at[k, off - 1], sems[3].at[k, off - 1],
                {"dp": 1 - dp},
            )
            c.start()
            halves.append(c)
    return halves


def gather_finish(copies, halves):
    for c in copies.values():
        c.wait_send()
    for c in halves:
        c.wait()


def halved(w):
    return w.reshape(2, w.shape[0] // 2, w.shape[1])


def stats_row(x):
    channels = x.shape[1]
    part = 1.0 / channels
    mean = dot(x, jnp.full((channels, channels), part, BF))
    square = jnp.square(x.astype(F32) - mean)
    high = square.astype(BF)
    low = (square - high.astype(F32)).astype(BF)
    ones = jnp.ones((8, channels), BF)
    rows = ((1,), (1,))
    mean_row = dot(jnp.full((8, channels), part, BF), x, rows)
    spread_row = dot(ones, high, rows) + dot(ones, low, rows)
    return mean_row[0:1], spread_row[0:1]


def block_kernel(
    size, factor, n_head, n_band,
    tok, gain, cr, cc, fr, taps, wq, wk, wv, wo,
    base, landed,
    xs, stat, stats, comb, halo, rim, edge, padded, side_comb, turned, table, part, arrived, whole,
    wide, query, gq, gk, gv, go, weight, sampled, flipped, keys, values, attended, mine,
    ssend, srecv, tsend, trecv, lsend, lrecv, esend, erecv, bsend, brecv, zsend, zrecv,
    asend, arecv, wsend, wrecv, dsend, drecv, osend, orecv,
):
    head, band, dp = (lax.axis_index(name) for name in ("head", "band", "dp"))
    bands, heads = range(1, n_band), range(1, n_head)
    places = [{"head": shift(head, off, n_head)} for off in heads]
    places += [{"band": shift(band, off, n_band)} for off in bands]
    places += [{"dp": 1 - dp}]
    rows, columns, channels = tok.shape
    margin = KER // 2
    per_head = rows // n_head
    side_pad = 8
    greet(places)

    sems = (wsend, wrecv, dsend, drecv)
    early = [(0, wq, gq)]
    later = [(1, wk, gk), (2, wv, gv)]
    last = [(3, wo, go)]
    copies = gather_start(early, head, dp, n_head, sems)
    after = {"band": shift(band, 1, n_band)}
    before = {"band": shift(band, n_band - 1, n_band)}
    up = remote(tok.at[pl.ds(rows - margin, margin)], halo.at[0], lsend.at[0], lrecv.at[0], after)
    down = remote(tok.at[pl.ds(0, margin)], halo.at[1], lsend.at[1], lrecv.at[1], before)

    @pl.when(band < n_band - 1)
    def _():
        up.start()

    @pl.when(band > 0)
    def _():
        down.start()

    for r in range(rows):
        mean, spread = stats_row(tok[r])
        stat[0:1, r * columns : (r + 1) * columns] = mean
        stat[1:2, r * columns : (r + 1) * columns] = spread
    told, moved = [], []
    for off in heads:
        c = remote(
            stat, stats.at[head], ssend.at[off - 1], srecv.at[off - 1],
            {"head": shift(head, off, n_head)},
        )
        c.start()
        told.append(c)
    for off in heads:
        to = shift(head, off, n_head)
        c = remote(
            tok.at[pl.ds(to * per_head, per_head)], xs.at[head], tsend.at[off - 1],
            trecv.at[off - 1], {"head": to},
        )
        c.start()
        moved.append(c)
    copies.update(gather_start(later, head, dp, n_head, sems))
    stats[head] = stat[...]
    xs[head] = tok[pl.ds(head * per_head, per_head)]

    left = (1.0 - fr[1:2]).astype(BF).astype(F32)
    right = fr[1:2].astype(BF).astype(F32)
    top = (1.0 - fr[0:1]).astype(BF).astype(F32)
    bottom = fr[0:1].astype(BF).astype(F32)
    points = cc.shape[1]
    share = channels // n_band
    chunk = 256
    for begin in range(0, points, chunk):
        at = slice(begin, begin + chunk)
        spot = lax.broadcasted_iota(jnp.int32, (columns, chunk), 0)
        table[:, at] = jnp.where(
            spot == cc[:, at], left[:, at], jnp.where(spot == cc[:, at] + 1, right[:, at], 0.0)
        ).astype(BF)
    padded[:, 0:side_pad, :] = jnp.zeros((rows + 2 * margin, side_pad, channels), F32)
    padded[:, side_pad + columns :, :] = jnp.zeros((rows + 2 * margin, side_pad, channels), F32)
    comb[...] = jnp.zeros_like(comb)
    side_comb[...] = jnp.zeros_like(side_comb)

    for c in told:
        c.wait()
    mean = stats[0, 0:1]
    for i in range(1, n_head):
        mean = mean + stats[i, 0:1]
    mean = mean * (1.0 / n_head)
    total = jnp.zeros_like(mean)
    for i in range(n_head):
        total = total + stats[i, 1:2] + channels * jnp.square(stats[i, 0:1] - mean)
    comb[0:1, :] = mean
    comb[1:2, :] = lax.rsqrt(total * (1.0 / (n_head * channels)) + EPS)
    edge[0] = comb[0:2, (rows - margin) * columns :]
    edge[1] = comb[0:2, : margin * columns]
    rim_up = remote(edge.at[0], rim.at[0], esend.at[0], erecv.at[0], after)
    rim_down = remote(edge.at[1], rim.at[1], esend.at[1], erecv.at[1], before)
    rim_up.start()
    rim_down.start()
    for r in range(rows):
        col = comb[:, r * columns : (r + 1) * columns].T
        value = ((tok[r].astype(F32) - col[:, 0:1]) * col[:, 1:2] * gain[head]).astype(BF)
        padded[margin + r, side_pad : side_pad + columns, :] = value.astype(F32)
        turned[r * channels : (r + 1) * channels, :] = value.T
    for begin in range(0, points, chunk):
        at = slice(begin, begin + chunk)
        inner = dot(turned[...], table[:, at])
        total = jnp.zeros((channels, chunk), F32)
        for r in range(rows):
            row = band * rows + r
            w = jnp.where(cr[:, at] == row, top[:, at], 0.0) + jnp.where(
                cr[:, at] + 1 == row, bottom[:, at], 0.0
            )
            total = total + w * inner[r * channels : (r + 1) * channels]
        for b in range(n_band):
            part[b, :, at] = total[b * share : (b + 1) * share].astype(BF)
    parts = []
    for off in bands:
        to = shift(band, off, n_band)
        c = remote(part.at[to], arrived.at[off - 1], bsend.at[off - 1], brecv.at[off - 1], {"band": to})
        c.start()
        parts.append(c)

    def fill(side):
        side_comb[0:2, :] = rim[side]
        there = band > 0 if side == 0 else band < n_band - 1
        for r in range(margin):
            col = side_comb[:, r * columns : (r + 1) * columns].T
            value = (halo[side, r].astype(F32) - col[:, 0:1]) * col[:, 1:2] * gain[head]
            value = jnp.where(there, value.astype(BF).astype(F32), 0.0)
            padded[side * (margin + rows) + r, side_pad : side_pad + columns, :] = value

    tile = 64

    def convolve(first, end):
        @pl.loop(first, end)
        def _(r):
            @pl.loop(0, columns // tile)
            def _(step):
                begin = pl.multiple_of(step * tile, tile)
                at = pl.ds(begin, tile)
                total = tok[r, at, :].astype(F32)
                for a in range(KER):
                    for b in range(KER):
                        total = total + taps[a * KER + b : a * KER + b + 1, :] * padded[
                            r + a, pl.ds(begin + (side_pad - margin + b), tile), :
                        ]
                base[r, at, :] = total

    rim_up.wait()
    rim_down.wait()

    @pl.when(band < n_band - 1)
    def _():
        up.wait_send()
        down.wait_recv()

    @pl.when(band > 0)
    def _():
        down.wait_send()
        up.wait_recv()

    fill(0)
    fill(1)
    convolve(0, rows // 4)

    total = part[band].astype(F32)
    for off in bands:
        parts[off - 1].wait_recv()
        total = total + arrived[off - 1].astype(F32)
    whole[band, head] = total.astype(BF)
    along, across = [], []
    for off in bands:
        c = remote(
            whole.at[band, head], whole.at[band, head], zsend.at[off - 1], zrecv.at[off - 1],
            {"band": shift(band, off, n_band)},
        )
        c.start()
        along.append(c)
    for step in range(n_band):
        source = shift(band, n_band - step, n_band)
        if step == 1:
            convolve(rows // 4, rows // 2)
        if step:
            along[step - 1].wait_recv()
        for off in heads:
            c = remote(
                whole.at[source, head], whole.at[source, head], asend.at[step, off - 1],
                arecv.at[step, off - 1], {"head": shift(head, off, n_head)},
            )
            c.start()
            across.append(c)
    copies.update(gather_start(last, head, dp, n_head, sems))
    halves = gather_relay(early + later, copies, head, dp, n_head, sems)
    convolve(rows // 2, rows)

    for c in moved:
        c.wait()
    per = per_head * columns
    for r in range(per_head):
        begin = pl.multiple_of(head * per + r * columns, 128)
        col = comb[:, pl.ds(begin, columns)].T
        for i in range(n_head):
            value = (xs[i, r].astype(F32) - col[:, 0:1]) * col[:, 1:2] * gain[i]
            wide[r * columns : (r + 1) * columns, i * channels : (i + 1) * channels] = value.astype(BF)
    for c in halves:
        c.wait()
    half = gq.shape[2]
    for a in range(2):
        for i in range(n_head):
            weight[a * half : (a + 1) * half, i * channels : (i + 1) * channels] = gq[a, i]

    @pl.loop(0, per // 256)
    def _(step):
        at = pl.ds(pl.multiple_of(step * 256, 256), 256)
        query[at, :] = (dot(wide[at, :], weight[...]) * factor).astype(BF)

    for c in across:
        c.wait()
    for c in along + parts:
        c.wait_send()

    group = channels // size
    for b in range(n_band):
        for i in range(n_head):
            at = i * channels + b * share
            sampled[at : at + share, :] = whole[b, i]
    flipped[...] = sampled[...].T

    @pl.loop(0, n_head)
    def _(i):
        flip = ((0,), (0,))
        key = dot(gk[0, i], sampled[0:half, :], flip) + dot(gk[1, i], sampled[half:, :], flip)
        value = dot(flipped[:, 0:half], gv[0, i]) + dot(flipped[:, half:], gv[1, i])
        key_spot = lax.broadcasted_iota(jnp.int32, key.shape, 0)
        value_spot = lax.broadcasted_iota(jnp.int32, value.shape, 1)
        for j in range(group):
            low_end, high_end = j * size, (j + 1) * size
            keep = (key_spot >= low_end) & (key_spot < high_end)
            keys[i * group + j] = jnp.where(keep, key, 0.0).astype(BF)
            keep = (value_spot >= low_end) & (value_spot < high_end)
            values[i * group + j, :, 0:channels] = jnp.where(keep, value, 0.0).astype(BF)
            values[i * group + j, :, channels:] = jnp.ones((points, channels), BF)

    halves = gather_relay(last, copies, head, dp, n_head, sems)
    gather_finish(copies, halves)
    low = go.shape[2]
    for a in range(2):
        for i in range(n_head):
            at = i * channels + a * low
            weight[at : at + low, :] = go[a, i]
    block = attended.shape[0]
    steps = query.shape[0] // block

    def back(step, off):
        at = pl.ds(pl.multiple_of(step * block, block), block)
        to = shift(head, off, n_head)
        return remote(
            mine.at[to, at], landed.at[head, at], osend.at[step, off - 1], orecv.at[step, off - 1],
            {"head": to},
        )

    @pl.loop(0, steps)
    def _(step):
        at = pl.ds(pl.multiple_of(step * block, block), block)

        def score(h):
            i = h // group
            return dot(query[at, i * channels : (i + 1) * channels], keys[h])

        following = score(0)
        for i in range(n_head):
            total = jnp.zeros((block, channels), F32)
            for j in range(group):
                h = i * group + j
                current = following
                if h + 1 < n_head * group:
                    following = score(h + 1)
                top = jnp.max(current, axis=1, keepdims=True)
                prob = jnp.exp2(current - top).astype(BF)
                both = dot(prob, values[h])
                total = total + both[:, 0:channels] / both[:, channels:]
            attended[:, i * channels : (i + 1) * channels] = total.astype(BF)
        result = dot(attended[...], weight[...])
        for i in range(n_head):
            mine[i, at, :] = result[:, i * channels : (i + 1) * channels].astype(BF)
        for off in heads:
            back(step, off).start()

    landed[head] = mine[head]
    for off in heads:
        for step in range(steps):
            back(step, off).wait()


def run_block(tokens, gain, cr, cc, fr, taps, wq, wk, wv, wo, n_head, n_band):
    rows, columns, channels = tokens.shape
    width = n_head * channels
    size = width // HEADS
    points = cc.shape[1]
    share = channels // n_band
    margin = KER // 2
    per_head = rows // n_head
    count = per_head * columns
    block = 256
    weights = [halved(w) for w in (wq, wk, wv, wo)]
    factor = math.log2(math.e) / math.sqrt(size)
    V = pltpu.VMEM
    sem = pltpu.SemaphoreType.DMA
    scratch = [
        V((n_head, per_head, columns, channels), BF),
        V((2, rows * columns), F32),
        V((n_head, 2, rows * columns), F32),
        V((8, rows * columns), F32),
        V((2, margin, columns, channels), BF),
        V((2, 2, margin * columns), F32),
        V((2, 2, margin * columns), F32),
        V((rows + 2 * margin, columns + 16, channels), F32),
        V((8, margin * columns), F32),
        V((rows * channels, columns), BF),
        V((columns, points), BF),
        V((n_band, share, points), BF),
        V((n_band - 1, share, points), BF),
        V((n_band, n_head, share, points), BF),
        V((count, width), BF),
        V((count, width), BF),
    ]
    scratch += [V((2, n_head) + w.shape[1:], BF) for w in weights]
    scratch += [
        V((width, width), BF),
        V((width, points), BF),
        V((points, width), BF),
        V((HEADS, channels, points), BF),
        V((HEADS, points, 2 * channels), BF),
        V((block, width), BF),
        V((n_head, count, channels), BF),
    ]
    for shape in (
        (n_head - 1,), (n_head - 1,), (2,), (2,), (n_band - 1,), (n_band - 1,),
        (n_band, n_head - 1), (4, n_head - 1), (4, n_head - 1), (count // block, n_head - 1),
    ):
        scratch += [sem(shape)] * 2
    return pl.pallas_call(
        functools.partial(block_kernel, size, factor, n_head, n_band),
        out_shape=[
            jax.ShapeDtypeStruct(tokens.shape, F32),
            jax.ShapeDtypeStruct((n_head, count, channels), BF),
        ],
        in_specs=[VM] * 10,
        out_specs=[VM] * 2,
        scratch_shapes=scratch,
        compiler_params=params(collective_id=0, has_side_effects=True),
        name="block",
    )(tokens, gain, cr, cc, fr, taps, *weights)


def shards(
    tokens, corner_row, corner_col, fraction, w_query, w_key, w_value, w_out, conv_kernel, norm_gain
):
    n_head, n_band = lax.axis_size("head"), lax.axis_size("band")
    channels = tokens.shape[2]
    base, projected = run_block(
        tokens, norm_gain.reshape(n_head, 1, channels), corner_row[None], corner_col[None], fraction,
        conv_kernel, w_query, w_key, w_value, w_out, n_head, n_band,
    )
    return (base + projected.reshape(tokens.shape).astype(F32)).astype(BF)


def solution(mesh):
    return jax.shard_map(
        shards,
        mesh=mesh,
        in_specs=(
            P(("dp", "band"), None, "head"),
            P("dp"),
            P("dp"),
            P(None, "dp"),
            P(None, "head"),
            P(None, "head"),
            P(None, "head"),
            P("head", None),
            P(None, "head"),
            P(),
        ),
        out_specs=P(("dp", "band"), None, "head"),
        check_vma=False,
    )
```

```python
import functools
import math

import jax
import jax.numpy as jnp
from jax import lax
from jax.experimental import pallas as pl
from jax.experimental.pallas import tpu as pltpu
from jax.sharding import PartitionSpec as P

HEADS = 16
KER = 5
EPS = 1e-05
BF = jnp.bfloat16
F32 = jnp.float32
VM = pl.BlockSpec(memory_space=pltpu.VMEM)


def params(**more):
    return pltpu.CompilerParams(vmem_limit_bytes=60 * 1024 * 1024, **more)


def dot(a, b, dims=((1,), (0,))):
    return lax.dot_general(a, b, (dims, ((), ())), preferred_element_type=F32)


def shift(me, off, count):
    return lax.rem(me + off, count)


def remote(src, dst, send, recv, where):
    return pltpu.make_async_remote_copy(
        src_ref=src,
        dst_ref=dst,
        send_sem=send,
        recv_sem=recv,
        device_id=where,
        device_id_type=pl.DeviceIdType.MESH,
    )


def greet(places):
    barrier = pltpu.get_barrier_semaphore()
    for where in places:
        pl.semaphore_signal(barrier, inc=1, device_id=where, device_id_type=pl.DeviceIdType.MESH)
    pl.semaphore_wait(barrier, len(places))


def gather_start(pairs, head, dp, n_head, sems):
    copies = {}
    for off in range(1, n_head):
        to = shift(head, off, n_head)
        for k, src, dst in pairs:
            c = remote(src.at[dp], dst.at[dp, head], sems[0].at[k, off - 1], sems[1].at[k, off - 1], {"head": to})
            c.start()
            copies[k, off] = c
    return copies


def gather_relay(pairs, copies, head, dp, n_head, sems):
    halves = []
    for off in range(1, n_head):
        back = shift(head, n_head - off, n_head)
        for k, src, dst in pairs:
            copies[k, off].wait_recv()
            c = remote(
                dst.at[dp, back], dst.at[dp, back], sems[2].at[k, off - 1], sems[3].at[k, off - 1],
                {"dp": 1 - dp},
            )
            c.start()
            halves.append(c)
    return halves


def gather_finish(copies, halves):
    for c in copies.values():
        c.wait_send()
    for c in halves:
        c.wait()


def halved(w):
    return w.reshape(2, w.shape[0] // 2, w.shape[1])


def stats_row(x):
    channels = x.shape[1]
    part = 1.0 / channels
    mean = dot(x, jnp.full((channels, channels), part, BF))
    square = jnp.square(x.astype(F32) - mean)
    high = square.astype(BF)
    low = (square - high.astype(F32)).astype(BF)
    ones = jnp.ones((8, channels), BF)
    rows = ((1,), (1,))
    mean_row = dot(jnp.full((8, channels), part, BF), x, rows)
    spread_row = dot(ones, high, rows) + dot(ones, low, rows)
    return mean_row[0:1], spread_row[0:1]


def block_kernel(
    size, factor, n_head, n_band,
    tok_in, gain_in, cr_in, cc_in, fr_in, taps_in, wq, wk, wv, wo,
    base_out, landed,
    tok, gain, cr, cc, fr, taps, base, xs, stat, stats, comb, halo, rim, edge, padded, side_comb, turned, table, part, arrived, whole,
    wide, query, gq, gk, gv, go, weight, sampled, flipped, keys, values, attended, mine,
    ssend, srecv, tsend, trecv, lsend, lrecv, esend, erecv, bsend, brecv, zsend, zrecv,
    asend, arecv, wsend, wrecv, dsend, drecv, osend, orecv, load_sem, own_sem, out_sem,
):
    head, band, dp = (lax.axis_index(name) for name in ("head", "band", "dp"))
    bands, heads = range(1, n_band), range(1, n_head)
    places = [{"head": shift(head, off, n_head)} for off in heads]
    places += [{"band": shift(band, off, n_band)} for off in bands]
    places += [{"dp": 1 - dp}]
    rows, columns, channels = tok.shape
    margin = KER // 2
    per_head = rows // n_head
    side_pad = 8
    inputs = [(tok_in, tok), (gain_in, gain), (cr_in, cr), (cc_in, cc), (fr_in, fr), (taps_in, taps)]
    loads = [pltpu.make_async_copy(src, dst, load_sem.at[k]) for k, (src, dst) in enumerate(inputs)]
    owns = [
        pltpu.make_async_copy(src.at[side], dst.at[side, head], own_sem.at[2 * k + side])
        for k, (src, dst) in enumerate([(wq, gq), (wk, gk), (wv, gv), (wo, go)])
        for side in range(2)
    ]
    for c in loads + owns:
        c.start()
    greet(places)

    sems = (wsend, wrecv, dsend, drecv)
    early = [(0, wq, gq)]
    later = [(1, wk, gk), (2, wv, gv)]
    last = [(3, wo, go)]
    copies = gather_start(early, head, dp, n_head, sems)
    after = {"band": shift(band, 1, n_band)}
    before = {"band": shift(band, n_band - 1, n_band)}
    up = remote(tok_in.at[pl.ds(rows - margin, margin)], halo.at[0], lsend.at[0], lrecv.at[0], after)
    down = remote(tok_in.at[pl.ds(0, margin)], halo.at[1], lsend.at[1], lrecv.at[1], before)

    @pl.when(band < n_band - 1)
    def _():
        up.start()

    @pl.when(band > 0)
    def _():
        down.start()

    for c in loads:
        c.wait()
    for r in range(rows):
        mean, spread = stats_row(tok[r])
        stat[0:1, r * columns : (r + 1) * columns] = mean
        stat[1:2, r * columns : (r + 1) * columns] = spread
    told, moved = [], []
    for off in heads:
        c = remote(
            stat, stats.at[head], ssend.at[off - 1], srecv.at[off - 1],
            {"head": shift(head, off, n_head)},
        )
        c.start()
        told.append(c)
    for off in heads:
        to = shift(head, off, n_head)
        c = remote(
            tok_in.at[pl.ds(to * per_head, per_head)], xs.at[head], tsend.at[off - 1],
            trecv.at[off - 1], {"head": to},
        )
        c.start()
        moved.append(c)
    copies.update(gather_start(later, head, dp, n_head, sems))
    stats[head] = stat[...]
    xs[head] = tok[pl.ds(head * per_head, per_head)]

    left = (1.0 - fr[1:2]).astype(BF).astype(F32)
    right = fr[1:2].astype(BF).astype(F32)
    top = (1.0 - fr[0:1]).astype(BF).astype(F32)
    bottom = fr[0:1].astype(BF).astype(F32)
    points = cc.shape[1]
    share = channels // n_band
    chunk = 256
    for begin in range(0, points, chunk):
        at = slice(begin, begin + chunk)
        spot = lax.broadcasted_iota(jnp.int32, (columns, chunk), 0)
        table[:, at] = jnp.where(
            spot == cc[:, at], left[:, at], jnp.where(spot == cc[:, at] + 1, right[:, at], 0.0)
        ).astype(BF)
    padded[:, 0:side_pad, :] = jnp.zeros((rows + 2 * margin, side_pad, channels), F32)
    padded[:, side_pad + columns :, :] = jnp.zeros((rows + 2 * margin, side_pad, channels), F32)
    comb[...] = jnp.zeros_like(comb)
    side_comb[...] = jnp.zeros_like(side_comb)

    for c in owns + told:
        c.wait()
    mean = stats[0, 0:1]
    for i in range(1, n_head):
        mean = mean + stats[i, 0:1]
    mean = mean * (1.0 / n_head)
    total = jnp.zeros_like(mean)
    for i in range(n_head):
        total = total + stats[i, 1:2] + channels * jnp.square(stats[i, 0:1] - mean)
    comb[0:1, :] = mean
    comb[1:2, :] = lax.rsqrt(total * (1.0 / (n_head * channels)) + EPS)
    edge[0] = comb[0:2, (rows - margin) * columns :]
    edge[1] = comb[0:2, : margin * columns]
    rim_up = remote(edge.at[0], rim.at[0], esend.at[0], erecv.at[0], after)
    rim_down = remote(edge.at[1], rim.at[1], esend.at[1], erecv.at[1], before)
    rim_up.start()
    rim_down.start()
    for r in range(rows):
        col = comb[:, r * columns : (r + 1) * columns].T
        value = ((tok[r].astype(F32) - col[:, 0:1]) * col[:, 1:2] * gain[head]).astype(BF)
        padded[margin + r, side_pad : side_pad + columns, :] = value.astype(F32)
        turned[r * channels : (r + 1) * channels, :] = value.T
    for begin in range(0, points, chunk):
        at = slice(begin, begin + chunk)
        inner = dot(turned[...], table[:, at])
        total = jnp.zeros((channels, chunk), F32)
        for r in range(rows):
            row = band * rows + r
            w = jnp.where(cr[:, at] == row, top[:, at], 0.0) + jnp.where(
                cr[:, at] + 1 == row, bottom[:, at], 0.0
            )
            total = total + w * inner[r * channels : (r + 1) * channels]
        for b in range(n_band):
            part[b, :, at] = total[b * share : (b + 1) * share].astype(BF)
    parts = []
    for off in bands:
        to = shift(band, off, n_band)
        c = remote(part.at[to], arrived.at[off - 1], bsend.at[off - 1], brecv.at[off - 1], {"band": to})
        c.start()
        parts.append(c)

    def fill(side):
        side_comb[0:2, :] = rim[side]
        there = band > 0 if side == 0 else band < n_band - 1
        for r in range(margin):
            col = side_comb[:, r * columns : (r + 1) * columns].T
            value = (halo[side, r].astype(F32) - col[:, 0:1]) * col[:, 1:2] * gain[head]
            value = jnp.where(there, value.astype(BF).astype(F32), 0.0)
            padded[side * (margin + rows) + r, side_pad : side_pad + columns, :] = value

    tile = 64

    def convolve(first, end):
        @pl.loop(first, end)
        def _(r):
            @pl.loop(0, columns // tile)
            def _(step):
                begin = pl.multiple_of(step * tile, tile)
                at = pl.ds(begin, tile)
                total = tok[r, at, :].astype(F32)
                for a in range(KER):
                    for b in range(KER):
                        total = total + taps[a * KER + b : a * KER + b + 1, :] * padded[
                            r + a, pl.ds(begin + (side_pad - margin + b), tile), :
                        ]
                base[r, at, :] = total

    rim_up.wait()
    rim_down.wait()

    @pl.when(band < n_band - 1)
    def _():
        up.wait_send()
        down.wait_recv()

    @pl.when(band > 0)
    def _():
        down.wait_send()
        up.wait_recv()

    fill(0)
    fill(1)
    convolve(0, rows // 4)

    total = part[band].astype(F32)
    for off in bands:
        parts[off - 1].wait_recv()
        total = total + arrived[off - 1].astype(F32)
    whole[band, head] = total.astype(BF)
    along, across = [], []
    for off in bands:
        c = remote(
            whole.at[band, head], whole.at[band, head], zsend.at[off - 1], zrecv.at[off - 1],
            {"band": shift(band, off, n_band)},
        )
        c.start()
        along.append(c)
    for step in range(n_band):
        source = shift(band, n_band - step, n_band)
        if step == 1:
            convolve(rows // 4, rows // 2)
        if step:
            along[step - 1].wait_recv()
        for off in heads:
            c = remote(
                whole.at[source, head], whole.at[source, head], asend.at[step, off - 1],
                arecv.at[step, off - 1], {"head": shift(head, off, n_head)},
            )
            c.start()
            across.append(c)
    copies.update(gather_start(last, head, dp, n_head, sems))
    halves = gather_relay(early + later, copies, head, dp, n_head, sems)
    convolve(rows // 2, rows)
    base_copy = pltpu.make_async_copy(base, base_out, out_sem.at[0])
    base_copy.start()

    @pl.loop(0, n_head * (channels // size))
    def _(h):
        values[h, :, channels:] = jnp.ones((points, channels), BF)

    for c in moved:
        c.wait()
    per = per_head * columns
    for r in range(per_head):
        begin = pl.multiple_of(head * per + r * columns, 128)
        col = comb[:, pl.ds(begin, columns)].T
        for i in range(n_head):
            value = (xs[i, r].astype(F32) - col[:, 0:1]) * col[:, 1:2] * gain[i]
            wide[r * columns : (r + 1) * columns, i * channels : (i + 1) * channels] = value.astype(BF)
    for c in halves:
        c.wait()
    half = gq.shape[2]
    for a in range(2):
        for i in range(n_head):
            weight[a * half : (a + 1) * half, i * channels : (i + 1) * channels] = gq[a, i]

    @pl.loop(0, per // 256)
    def _(step):
        at = pl.ds(pl.multiple_of(step * 256, 256), 256)
        query[at, :] = (dot(wide[at, :], weight[...]) * factor).astype(BF)

    for c in across:
        c.wait()
    for c in along + parts:
        c.wait_send()

    group = channels // size
    for b in range(n_band):
        for i in range(n_head):
            at = i * channels + b * share
            sampled[at : at + share, :] = whole[b, i]
    flipped[...] = sampled[...].T

    @pl.loop(0, n_head)
    def _(i):
        flip = ((0,), (0,))
        key = dot(gk[0, i], sampled[0:half, :], flip) + dot(gk[1, i], sampled[half:, :], flip)
        value = dot(flipped[:, 0:half], gv[0, i]) + dot(flipped[:, half:], gv[1, i])
        key_spot = lax.broadcasted_iota(jnp.int32, key.shape, 0)
        value_spot = lax.broadcasted_iota(jnp.int32, value.shape, 1)
        for j in range(group):
            low_end, high_end = j * size, (j + 1) * size
            keep = (key_spot >= low_end) & (key_spot < high_end)
            keys[i * group + j] = jnp.where(keep, key, 0.0).astype(BF)
            keep = (value_spot >= low_end) & (value_spot < high_end)
            values[i * group + j, :, 0:channels] = jnp.where(keep, value, 0.0).astype(BF)

    halves = gather_relay(last, copies, head, dp, n_head, sems)
    gather_finish(copies, halves)
    low = go.shape[2]
    for a in range(2):
        for i in range(n_head):
            at = i * channels + a * low
            weight[at : at + low, :] = go[a, i]
    block = attended.shape[0]
    steps = query.shape[0] // block

    def back(step, off):
        at = pl.ds(pl.multiple_of(step * block, block), block)
        to = shift(head, off, n_head)
        return remote(
            mine.at[to, at], landed.at[head, at], osend.at[step, off - 1], orecv.at[step, off - 1],
            {"head": to},
        )

    @pl.loop(0, steps)
    def _(step):
        at = pl.ds(pl.multiple_of(step * block, block), block)

        def score(h):
            i = h // group
            return dot(query[at, i * channels : (i + 1) * channels], keys[h])

        following = score(0)
        for i in range(n_head):
            total = jnp.zeros((block, channels), F32)
            for j in range(group):
                h = i * group + j
                current = following
                if h + 1 < n_head * group:
                    following = score(h + 1)
                top = jnp.max(current, axis=1, keepdims=True)
                prob = jnp.exp2(current - top).astype(BF)
                both = dot(prob, values[h])
                total = total + both[:, 0:channels] / both[:, channels:]
            attended[:, i * channels : (i + 1) * channels] = total.astype(BF)
        result = dot(attended[...], weight[...])
        for i in range(n_head):
            mine[i, at, :] = result[:, i * channels : (i + 1) * channels].astype(BF)
        for off in heads:
            back(step, off).start()

    own_copy = pltpu.make_async_copy(mine.at[head], landed.at[head], out_sem.at[1])
    own_copy.start()
    base_copy.wait()
    for off in heads:
        for step in range(steps):
            back(step, off).wait()
    own_copy.wait()


def run_block(tokens, gain, cr, cc, fr, taps, wq, wk, wv, wo, n_head, n_band):
    rows, columns, channels = tokens.shape
    width = n_head * channels
    size = width // HEADS
    points = cc.shape[1]
    share = channels // n_band
    margin = KER // 2
    per_head = rows // n_head
    count = per_head * columns
    block = 256
    weights = [halved(w) for w in (wq, wk, wv, wo)]
    factor = math.log2(math.e) / math.sqrt(size)
    V = pltpu.VMEM
    sem = pltpu.SemaphoreType.DMA
    inputs = (tokens, gain, cr, cc, fr, taps)
    scratch = [V(x.shape, x.dtype) for x in inputs]
    scratch += [
        V(tokens.shape, F32),
        V((n_head, per_head, columns, channels), BF),
        V((2, rows * columns), F32),
        V((n_head, 2, rows * columns), F32),
        V((8, rows * columns), F32),
        V((2, margin, columns, channels), BF),
        V((2, 2, margin * columns), F32),
        V((2, 2, margin * columns), F32),
        V((rows + 2 * margin, columns + 16, channels), F32),
        V((8, margin * columns), F32),
        V((rows * channels, columns), BF),
        V((columns, points), BF),
        V((n_band, share, points), BF),
        V((n_band - 1, share, points), BF),
        V((n_band, n_head, share, points), BF),
        V((count, width), BF),
        V((count, width), BF),
    ]
    scratch += [V((2, n_head) + w.shape[1:], BF) for w in weights]
    scratch += [
        V((width, width), BF),
        V((width, points), BF),
        V((points, width), BF),
        V((HEADS, channels, points), BF),
        V((HEADS, points, 2 * channels), BF),
        V((block, width), BF),
        V((n_head, count, channels), BF),
    ]
    for shape in (
        (n_head - 1,), (n_head - 1,), (2,), (2,), (n_band - 1,), (n_band - 1,),
        (n_band, n_head - 1), (4, n_head - 1), (4, n_head - 1), (count // block, n_head - 1),
    ):
        scratch += [sem(shape)] * 2
    scratch += [sem((len(inputs),)), sem((2 * len(weights),)), sem((2,))]
    return pl.pallas_call(
        functools.partial(block_kernel, size, factor, n_head, n_band),
        out_shape=[
            jax.ShapeDtypeStruct(tokens.shape, F32),
            jax.ShapeDtypeStruct((n_head, count, channels), BF),
        ],
        in_specs=[pl.BlockSpec(memory_space=pltpu.HBM)] * 10,
        out_specs=[pl.BlockSpec(memory_space=pltpu.HBM)] * 2,
        scratch_shapes=scratch,
        compiler_params=params(collective_id=0, has_side_effects=True),
        name="block",
    )(tokens, gain, cr, cc, fr, taps, *weights)


def shards(
    tokens, corner_row, corner_col, fraction, w_query, w_key, w_value, w_out, conv_kernel, norm_gain
):
    n_head, n_band = lax.axis_size("head"), lax.axis_size("band")
    channels = tokens.shape[2]
    base, projected = run_block(
        tokens, norm_gain.reshape(n_head, 1, channels), corner_row[None], corner_col[None], fraction,
        conv_kernel, w_query, w_key, w_value, w_out, n_head, n_band,
    )
    return (base + projected.reshape(tokens.shape).astype(F32)).astype(BF)


def solution(mesh):
    return jax.shard_map(
        shards,
        mesh=mesh,
        in_specs=(
            P(("dp", "band"), None, "head"),
            P("dp"),
            P("dp"),
            P(None, "dp"),
            P(None, "head"),
            P(None, "head"),
            P(None, "head"),
            P("head", None),
            P(None, "head"),
            P(),
        ),
        out_specs=P(("dp", "band"), None, "head"),
        check_vma=False,
    )
```

```python
import functools
import math

import jax
import jax.numpy as jnp
from jax import lax
from jax.experimental import pallas as pl
from jax.experimental.pallas import tpu as pltpu
from jax.sharding import PartitionSpec as P

HEADS = 16
KER = 5
EPS = 1e-05
BF = jnp.bfloat16
F32 = jnp.float32
VM = pl.BlockSpec(memory_space=pltpu.VMEM)


def params(**more):
    return pltpu.CompilerParams(vmem_limit_bytes=60 * 1024 * 1024, **more)


def dot(a, b, dims=((1,), (0,))):
    return lax.dot_general(a, b, (dims, ((), ())), preferred_element_type=F32)


def shift(me, off, count):
    return lax.rem(me + off, count)


def remote(src, dst, send, recv, where):
    return pltpu.make_async_remote_copy(
        src_ref=src,
        dst_ref=dst,
        send_sem=send,
        recv_sem=recv,
        device_id=where,
        device_id_type=pl.DeviceIdType.MESH,
    )


def greet(places):
    barrier = pltpu.get_barrier_semaphore()
    for where in places:
        pl.semaphore_signal(barrier, inc=1, device_id=where, device_id_type=pl.DeviceIdType.MESH)
    pl.semaphore_wait(barrier, len(places))


def gather_start(pairs, head, dp, n_head, sems):
    copies = {}
    for off in range(1, n_head):
        to = shift(head, off, n_head)
        for k, src, dst in pairs:
            c = remote(src.at[dp], dst.at[dp, head], sems[0].at[k, off - 1], sems[1].at[k, off - 1], {"head": to})
            c.start()
            copies[k, off] = c
    return copies


def gather_relay(pairs, copies, head, dp, n_head, sems):
    halves = []
    for off in range(1, n_head):
        back = shift(head, n_head - off, n_head)
        for k, src, dst in pairs:
            copies[k, off].wait_recv()
            c = remote(
                dst.at[dp, back], dst.at[dp, back], sems[2].at[k, off - 1], sems[3].at[k, off - 1],
                {"dp": 1 - dp},
            )
            c.start()
            halves.append(c)
    return halves


def gather_finish(copies, halves):
    for c in copies.values():
        c.wait_send()
    for c in halves:
        c.wait()


def halved(w):
    return w.reshape(2, w.shape[0] // 2, w.shape[1])


def stats_row(x):
    channels = x.shape[1]
    part = 1.0 / channels
    mean = dot(x, jnp.full((channels, channels), part, BF))
    square = jnp.square(x.astype(F32) - mean)
    high = square.astype(BF)
    low = (square - high.astype(F32)).astype(BF)
    ones = jnp.ones((8, channels), BF)
    rows = ((1,), (1,))
    mean_row = dot(jnp.full((8, channels), part, BF), x, rows)
    spread_row = dot(ones, high, rows) + dot(ones, low, rows)
    return mean_row[0:1], spread_row[0:1]


def block_kernel(
    size, factor, n_head, n_band,
    tok_in, gain_in, cr_in, cc_in, fr_in, taps_in, wq, wk, wv, wo,
    base_out, landed,
    tok, gain, cr, cc, fr, taps, base, xs, stat, stats, comb, halo, rim, edge, padded, side_comb, turned, table, part, arrived, whole,
    wide, query, gq, gk, gv, go, weight, sampled, flipped, keys, values, attended, mine,
    ssend, srecv, tsend, trecv, lsend, lrecv, esend, erecv, bsend, brecv, zsend, zrecv,
    asend, arecv, wsend, wrecv, dsend, drecv, osend, orecv, load_sem, own_sem, out_sem,
):
    head, band, dp = (lax.axis_index(name) for name in ("head", "band", "dp"))
    bands, heads = range(1, n_band), range(1, n_head)
    places = [{"head": shift(head, off, n_head)} for off in heads]
    places += [{"band": shift(band, off, n_band)} for off in bands]
    places += [{"dp": 1 - dp}]
    rows, columns, channels = tok.shape
    margin = KER // 2
    per_head = rows // n_head
    side_pad = 8
    inputs = [(tok_in, tok), (gain_in, gain), (cr_in, cr), (cc_in, cc), (fr_in, fr), (taps_in, taps)]
    loads = [pltpu.make_async_copy(src, dst, load_sem.at[k]) for k, (src, dst) in enumerate(inputs)]
    owns = [
        pltpu.make_async_copy(src.at[side], dst.at[side, head], own_sem.at[2 * k + side])
        for k, (src, dst) in enumerate([(wq, gq), (wk, gk), (wv, gv), (wo, go)])
        for side in range(2)
    ]
    for c in loads + owns:
        c.start()
    greet(places)

    sems = (wsend, wrecv, dsend, drecv)
    early = [(0, wq, gq)]
    later = [(1, wk, gk), (2, wv, gv)]
    last = [(3, wo, go)]
    copies = gather_start(early, head, dp, n_head, sems)
    after = {"band": shift(band, 1, n_band)}
    before = {"band": shift(band, n_band - 1, n_band)}
    up = remote(tok_in.at[pl.ds(rows - margin, margin)], halo.at[0], lsend.at[0], lrecv.at[0], after)
    down = remote(tok_in.at[pl.ds(0, margin)], halo.at[1], lsend.at[1], lrecv.at[1], before)

    @pl.when(band < n_band - 1)
    def _():
        up.start()

    @pl.when(band > 0)
    def _():
        down.start()

    for c in loads:
        c.wait()
    for r in range(rows):
        mean, spread = stats_row(tok[r])
        stat[0:1, r * columns : (r + 1) * columns] = mean
        stat[1:2, r * columns : (r + 1) * columns] = spread
    told, moved = [], []
    for off in heads:
        c = remote(
            stat, stats.at[head], ssend.at[off - 1], srecv.at[off - 1],
            {"head": shift(head, off, n_head)},
        )
        c.start()
        told.append(c)
    for off in heads:
        to = shift(head, off, n_head)
        c = remote(
            tok_in.at[pl.ds(to * per_head, per_head)], xs.at[head], tsend.at[off - 1],
            trecv.at[off - 1], {"head": to},
        )
        c.start()
        moved.append(c)
    copies.update(gather_start(later, head, dp, n_head, sems))
    stats[head] = stat[...]
    xs[head] = tok[pl.ds(head * per_head, per_head)]

    left = (1.0 - fr[1:2]).astype(BF).astype(F32)
    right = fr[1:2].astype(BF).astype(F32)
    top = (1.0 - fr[0:1]).astype(BF).astype(F32)
    bottom = fr[0:1].astype(BF).astype(F32)
    points = cc.shape[1]
    share = channels // n_band
    chunk = 256
    for begin in range(0, points, chunk):
        at = slice(begin, begin + chunk)
        spot = lax.broadcasted_iota(jnp.int32, (columns, chunk), 0)
        table[:, at] = jnp.where(
            spot == cc[:, at], left[:, at], jnp.where(spot == cc[:, at] + 1, right[:, at], 0.0)
        ).astype(BF)
    padded[:, 0:side_pad, :] = jnp.zeros((rows + 2 * margin, side_pad, channels), F32)
    padded[:, side_pad + columns :, :] = jnp.zeros((rows + 2 * margin, side_pad, channels), F32)
    comb[...] = jnp.zeros_like(comb)
    side_comb[...] = jnp.zeros_like(side_comb)

    for c in owns + told:
        c.wait()
    mean = stats[0, 0:1]
    for i in range(1, n_head):
        mean = mean + stats[i, 0:1]
    mean = mean * (1.0 / n_head)
    total = jnp.zeros_like(mean)
    for i in range(n_head):
        total = total + stats[i, 1:2] + channels * jnp.square(stats[i, 0:1] - mean)
    comb[0:1, :] = mean
    comb[1:2, :] = lax.rsqrt(total * (1.0 / (n_head * channels)) + EPS)
    edge[0] = comb[0:2, (rows - margin) * columns :]
    edge[1] = comb[0:2, : margin * columns]
    rim_up = remote(edge.at[0], rim.at[0], esend.at[0], erecv.at[0], after)
    rim_down = remote(edge.at[1], rim.at[1], esend.at[1], erecv.at[1], before)
    rim_up.start()
    rim_down.start()
    for r in range(rows):
        col = comb[:, r * columns : (r + 1) * columns].T
        value = ((tok[r].astype(F32) - col[:, 0:1]) * col[:, 1:2] * gain[head]).astype(BF)
        padded[margin + r, side_pad : side_pad + columns, :] = value.astype(F32)
        turned[r * channels : (r + 1) * channels, :] = value.T
    for begin in range(0, points, chunk):
        at = slice(begin, begin + chunk)
        inner = dot(turned[...], table[:, at])
        total = jnp.zeros((channels, chunk), F32)
        for r in range(rows):
            row = band * rows + r
            w = jnp.where(cr[:, at] == row, top[:, at], 0.0) + jnp.where(
                cr[:, at] + 1 == row, bottom[:, at], 0.0
            )
            total = total + w * inner[r * channels : (r + 1) * channels]
        for b in range(n_band):
            part[b, :, at] = total[b * share : (b + 1) * share].astype(BF)
    parts = []
    for off in bands:
        to = shift(band, off, n_band)
        c = remote(part.at[to], arrived.at[off - 1], bsend.at[off - 1], brecv.at[off - 1], {"band": to})
        c.start()
        parts.append(c)

    def fill(side):
        side_comb[0:2, :] = rim[side]
        there = band > 0 if side == 0 else band < n_band - 1
        for r in range(margin):
            col = side_comb[:, r * columns : (r + 1) * columns].T
            value = (halo[side, r].astype(F32) - col[:, 0:1]) * col[:, 1:2] * gain[head]
            value = jnp.where(there, value.astype(BF).astype(F32), 0.0)
            padded[side * (margin + rows) + r, side_pad : side_pad + columns, :] = value

    tile = 64

    def convolve(first, end):
        @pl.loop(first, end)
        def _(r):
            @pl.loop(0, columns // tile)
            def _(step):
                begin = pl.multiple_of(step * tile, tile)
                at = pl.ds(begin, tile)
                total = tok[r, at, :].astype(F32)
                for a in range(KER):
                    for b in range(KER):
                        total = total + taps[a * KER + b : a * KER + b + 1, :] * padded[
                            r + a, pl.ds(begin + (side_pad - margin + b), tile), :
                        ]
                base[r, at, :] = total.astype(BF)

    rim_up.wait()
    rim_down.wait()

    @pl.when(band < n_band - 1)
    def _():
        up.wait_send()
        down.wait_recv()

    @pl.when(band > 0)
    def _():
        down.wait_send()
        up.wait_recv()

    fill(0)
    fill(1)
    convolve(0, rows // 4)

    total = part[band].astype(F32)
    for off in bands:
        parts[off - 1].wait_recv()
        total = total + arrived[off - 1].astype(F32)
    whole[band, head] = total.astype(BF)
    along, across = [], []
    for off in bands:
        c = remote(
            whole.at[band, head], whole.at[band, head], zsend.at[off - 1], zrecv.at[off - 1],
            {"band": shift(band, off, n_band)},
        )
        c.start()
        along.append(c)
    for step in range(n_band):
        source = shift(band, n_band - step, n_band)
        if step == 1:
            convolve(rows // 4, rows // 2)
        if step:
            along[step - 1].wait_recv()
        for off in heads:
            c = remote(
                whole.at[source, head], whole.at[source, head], asend.at[step, off - 1],
                arecv.at[step, off - 1], {"head": shift(head, off, n_head)},
            )
            c.start()
            across.append(c)
    copies.update(gather_start(last, head, dp, n_head, sems))
    halves = gather_relay(early + later, copies, head, dp, n_head, sems)
    convolve(rows // 2, rows)
    base_copy = pltpu.make_async_copy(base, base_out, out_sem.at[0])
    base_copy.start()

    @pl.loop(0, n_head * (channels // size))
    def _(h):
        values[h, :, channels:] = jnp.ones((points, channels), BF)

    for c in moved:
        c.wait()
    per = per_head * columns
    for r in range(per_head):
        begin = pl.multiple_of(head * per + r * columns, 128)
        col = comb[:, pl.ds(begin, columns)].T
        for i in range(n_head):
            value = (xs[i, r].astype(F32) - col[:, 0:1]) * col[:, 1:2] * gain[i]
            wide[r * columns : (r + 1) * columns, i * channels : (i + 1) * channels] = value.astype(BF)
    for c in halves:
        c.wait()
    half = gq.shape[2]
    for a in range(2):
        for i in range(n_head):
            weight[a * half : (a + 1) * half, i * channels : (i + 1) * channels] = gq[a, i]

    @pl.loop(0, per // 256)
    def _(step):
        at = pl.ds(pl.multiple_of(step * 256, 256), 256)
        query[at, :] = (dot(wide[at, :], weight[...]) * factor).astype(BF)

    for c in across:
        c.wait()
    for c in along + parts:
        c.wait_send()

    group = channels // size
    for b in range(n_band):
        for i in range(n_head):
            at = i * channels + b * share
            sampled[at : at + share, :] = whole[b, i]
    flipped[...] = sampled[...].T

    @pl.loop(0, n_head)
    def _(i):
        flip = ((0,), (0,))
        key = dot(gk[0, i], sampled[0:half, :], flip) + dot(gk[1, i], sampled[half:, :], flip)
        value = dot(flipped[:, 0:half], gv[0, i]) + dot(flipped[:, half:], gv[1, i])
        key_spot = lax.broadcasted_iota(jnp.int32, key.shape, 0)
        value_spot = lax.broadcasted_iota(jnp.int32, value.shape, 1)
        for j in range(group):
            low_end, high_end = j * size, (j + 1) * size
            keep = (key_spot >= low_end) & (key_spot < high_end)
            keys[i * group + j] = jnp.where(keep, key, 0.0).astype(BF)
            keep = (value_spot >= low_end) & (value_spot < high_end)
            values[i * group + j, :, 0:channels] = jnp.where(keep, value, 0.0).astype(BF)

    halves = gather_relay(last, copies, head, dp, n_head, sems)
    gather_finish(copies, halves)
    low = go.shape[2]
    for a in range(2):
        for i in range(n_head):
            at = i * channels + a * low
            weight[at : at + low, :] = go[a, i]
    block = attended.shape[0]
    steps = query.shape[0] // block

    def back(step, off):
        at = pl.ds(pl.multiple_of(step * block, block), block)
        to = shift(head, off, n_head)
        return remote(
            mine.at[to, at], landed.at[head, at], osend.at[step, off - 1], orecv.at[step, off - 1],
            {"head": to},
        )

    @pl.loop(0, steps)
    def _(step):
        at = pl.ds(pl.multiple_of(step * block, block), block)

        def score(h):
            i = h // group
            return dot(query[at, i * channels : (i + 1) * channels], keys[h])

        following = score(0)
        for i in range(n_head):
            total = jnp.zeros((block, channels), F32)
            for j in range(group):
                h = i * group + j
                current = following
                if h + 1 < n_head * group:
                    following = score(h + 1)
                top = jnp.max(current, axis=1, keepdims=True)
                prob = jnp.exp2(current - top).astype(BF)
                both = dot(prob, values[h])
                total = total + both[:, 0:channels] / both[:, channels:]
            attended[:, i * channels : (i + 1) * channels] = total.astype(BF)
        result = dot(attended[...], weight[...])
        for i in range(n_head):
            mine[i, at, :] = result[:, i * channels : (i + 1) * channels].astype(BF)
        for off in heads:
            back(step, off).start()

    own_copy = pltpu.make_async_copy(mine.at[head], landed.at[head], out_sem.at[1])
    own_copy.start()
    base_copy.wait()
    for off in heads:
        for step in range(steps):
            back(step, off).wait()
    own_copy.wait()


def run_block(tokens, gain, cr, cc, fr, taps, wq, wk, wv, wo, n_head, n_band):
    rows, columns, channels = tokens.shape
    width = n_head * channels
    size = width // HEADS
    points = cc.shape[1]
    share = channels // n_band
    margin = KER // 2
    per_head = rows // n_head
    count = per_head * columns
    block = 256
    weights = [halved(w) for w in (wq, wk, wv, wo)]
    factor = math.log2(math.e) / math.sqrt(size)
    V = pltpu.VMEM
    sem = pltpu.SemaphoreType.DMA
    inputs = (tokens, gain, cr, cc, fr, taps)
    scratch = [V(x.shape, x.dtype) for x in inputs]
    scratch += [
        V(tokens.shape, BF),
        V((n_head, per_head, columns, channels), BF),
        V((2, rows * columns), F32),
        V((n_head, 2, rows * columns), F32),
        V((8, rows * columns), F32),
        V((2, margin, columns, channels), BF),
        V((2, 2, margin * columns), F32),
        V((2, 2, margin * columns), F32),
        V((rows + 2 * margin, columns + 16, channels), F32),
        V((8, margin * columns), F32),
        V((rows * channels, columns), BF),
        V((columns, points), BF),
        V((n_band, share, points), BF),
        V((n_band - 1, share, points), BF),
        V((n_band, n_head, share, points), BF),
        V((count, width), BF),
        V((count, width), BF),
    ]
    scratch += [V((2, n_head) + w.shape[1:], BF) for w in weights]
    scratch += [
        V((width, width), BF),
        V((width, points), BF),
        V((points, width), BF),
        V((HEADS, channels, points), BF),
        V((HEADS, points, 2 * channels), BF),
        V((block, width), BF),
        V((n_head, count, channels), BF),
    ]
    for shape in (
        (n_head - 1,), (n_head - 1,), (2,), (2,), (n_band - 1,), (n_band - 1,),
        (n_band, n_head - 1), (4, n_head - 1), (4, n_head - 1), (count // block, n_head - 1),
    ):
        scratch += [sem(shape)] * 2
    scratch += [sem((len(inputs),)), sem((2 * len(weights),)), sem((2,))]
    return pl.pallas_call(
        functools.partial(block_kernel, size, factor, n_head, n_band),
        out_shape=[
            jax.ShapeDtypeStruct(tokens.shape, BF),
            jax.ShapeDtypeStruct((n_head, count, channels), BF),
        ],
        in_specs=[pl.BlockSpec(memory_space=pltpu.HBM)] * 10,
        out_specs=[pl.BlockSpec(memory_space=pltpu.HBM)] * 2,
        scratch_shapes=scratch,
        compiler_params=params(collective_id=0, has_side_effects=True),
        name="block",
    )(tokens, gain, cr, cc, fr, taps, *weights)


def shards(
    tokens, corner_row, corner_col, fraction, w_query, w_key, w_value, w_out, conv_kernel, norm_gain
):
    n_head, n_band = lax.axis_size("head"), lax.axis_size("band")
    channels = tokens.shape[2]
    base, projected = run_block(
        tokens, norm_gain.reshape(n_head, 1, channels), corner_row[None], corner_col[None], fraction,
        conv_kernel, w_query, w_key, w_value, w_out, n_head, n_band,
    )
    return (base.astype(F32) + projected.reshape(tokens.shape).astype(F32)).astype(BF)


def solution(mesh):
    return jax.shard_map(
        shards,
        mesh=mesh,
        in_specs=(
            P(("dp", "band"), None, "head"),
            P("dp"),
            P("dp"),
            P(None, "dp"),
            P(None, "head"),
            P(None, "head"),
            P(None, "head"),
            P("head", None),
            P(None, "head"),
            P(),
        ),
        out_specs=P(("dp", "band"), None, "head"),
        check_vma=False,
    )
```
